768 devices in a mesh: gx: 12 (over z), gy: 64 (over y, x, core).
Axes of the slice: x: 4, y: 8, z: 12, core: 2. Of those that a mesh axis runs over, the one named last changes fastest.
Arguments:
- heat_source: float32 [8, 192, 49152], P(None, 'gx', 'gy'), may hold values from -90 to 90
- density: float32 [192, 49152], P('gx', 'gy'), may hold values from 0.3 to 1
Outputs:
- solution_field: float32 [8, 192, 49152], P(None, 'gx', 'gy')
- residual: float32 [8, 192, 49152], P(None, 'gx', 'gy')
The draws below stay inside these ranges and needn't reach their ends.
All inputs are finite; a program needn't handle non-finite values.
Results may differ from the reference program's by a relative error of at most 0.0003.
Values sent between devices are 32-bit elements; how exact they have to be, the bound alone decides.
A program may use at most 32 MiB of HBM per device.

```python
import jax
import jax.numpy as jnp
import numpy as np
from jax import lax

LOADS = 8
NZ = 96
ITERS = 2
NX = 192
NY = 512


def draw_heat_source(key, part):
    first_key = jax.random.fold_in(key, 0)
    along_x = jnp.arange(NX, dtype=jnp.float32) / NX
    along_y = (jnp.arange(NY * NZ) // NZ).astype(jnp.float32) / NY
    ramp = jnp.exp(jnp.log(3.0) * along_x)[:, None] * jnp.exp(jnp.log(3.0) * along_y)[None, :]
    base = jnp.clip(jax.random.normal(first_key, (LOADS, NX, NY * NZ), jnp.float32), -6.0, 6.0)
    return (base * ramp).astype(jnp.float32)


def steps_of(rng, dims, cuts, least, top_value):
    level = 1.0
    for dim, parts in cuts:
        steps = jax.random.uniform(jax.random.fold_in(jax.random.fold_in(rng, 6), dim), (parts,), jnp.float32, least / len(cuts), top_value / len(cuts))
        level = level * jnp.repeat(jnp.exp(steps), dims[dim] // parts).reshape((-1,) + (1,) * (len(dims) - 1 - dim))
    return level


def setup_inputs(seed: int = 0) -> dict:
    streams_of = jax.random.split(jax.random.key(seed), 3)
    return {
        "heat_source": draw_heat_source(jax.random.fold_in(streams_of[2], 71), 0),
        "density": jnp.clip(0.3 + 0.7 * jax.random.uniform(streams_of[1], (NX, NY * NZ), jnp.float32) ** steps_of(streams_of[1], (NX, NY * NZ), ((0, 12), (1, 64)), -0.2, 0.2), 0.3, 1.0),
    }


KMIN = 0.001


def stiffness():
    table = np.zeros((8, 8), np.float32)
    levels = [4.0, 0.0, -1.0, -1.0]
    for first in range(8):
        for second in range(8):
            differ = first ^ second
            apart = (differ & 1) + ((differ >> 1) & 1) + ((differ >> 2) & 1)
            table[first, second] = levels[apart] / 12.0
    return table


def corners():
    return [((corner >> 2) & 1, (corner >> 1) & 1, corner & 1) for corner in range(8)]


def conductance(density):
    return KMIN + (1.0 - KMIN) * (density * density * density)


def reference(heat_source, density):
    conduct = conductance(density).reshape(NX, NY, NZ)
    k_elem = jnp.asarray(stiffness())
    offsets = corners()

    def spread(elems):
        summed = jnp.zeros((NX + 1, NY + 1, NZ + 1), jnp.float32)
        for corner, (off_x, off_y, off_z) in enumerate(offsets):
            summed = summed.at[off_x:off_x + NX, off_y:off_y + NY, off_z:off_z + NZ].add(elems[corner])
        return summed[:NX, :NY, :NZ]

    precond = spread(jnp.broadcast_to(conduct * k_elem[0, 0], (8, NX, NY, NZ)))

    def operate(field):
        padded = jnp.pad(field, ((0, 1), (0, 1), (0, 1)))
        values = jnp.stack([padded[off_x:off_x + NX, off_y:off_y + NY, off_z:off_z + NZ] for (off_x, off_y, off_z) in offsets])
        elems = jnp.einsum("nm,mabc->nabc", k_elem, values, precision=lax.Precision.HIGHEST) * conduct
        return spread(elems)

    def solve(source):
        source = source.reshape(NX, NY, NZ)
        solution = jnp.zeros((NX, NY, NZ), jnp.float32)
        residual = source
        scaled = residual / precond
        direction = scaled
        rz_sum = jnp.sum(residual * scaled)
        for step in range(ITERS):
            image = operate(direction)
            alpha = rz_sum / jnp.sum(direction * image)
            solution = solution + alpha * direction
            residual = residual - alpha * image
            scaled = residual / precond
            rz_next = jnp.sum(residual * scaled)
            direction = scaled + (rz_next / rz_sum) * direction
            rz_sum = rz_next
        return solution.reshape(NX, NY * NZ), residual.reshape(NX, NY * NZ)

    solution_all, residual_all = lax.map(solve, heat_source)
    return solution_all, residual_all
```

```python
import functools

import jax
import jax.numpy as jnp
from jax import lax
from jax.experimental import pallas as pl
from jax.experimental.pallas import tpu as pltpu
from jax.sharding import PartitionSpec as P

NZ = 96
KMIN = 0.001
MESH = pl.DeviceIdType.MESH
LANES = 128
LOADS = 8
XC = 16
YC = 8
XN, YN = XC + 4, YC + 4
SIDES = [(dx, dy) for dx in (-1, 0, 1) for dy in (-1, 0, 1) if (dx, dy) != (0, 0)]

HEAT_FROM = {1: (XC, 2), 0: (2, XC), -1: (2, 2)}
HEAT_TO = {1: (0, 2), 0: (2, XC), -1: (XC + 2, 2)}
HEATY_FROM = {1: (YC, 2), 0: (2, YC), -1: (2, 2)}
HEATY_TO = {1: (0, 2), 0: (2, YC), -1: (YC + 2, 2)}
DENS_FROM = {1: (16, 8), 0: (8, 16), -1: (8, 8)}
DENS_TO = {1: (0, 8), 0: (8, 16), -1: (24, 8)}
DENSY_FROM = {1: (768, 384), 0: (384, 768), -1: (384, 256)}
DENSY_TO = {1: (0, 384), 0: (384, 768), -1: (1152, 256)}


TILES = YC * NZ // LANES
TILE_STEP = XC * TILES


def to_tiles(field):
    parts = field.reshape(LOADS, XC // 8, 8, TILES, LANES)
    return parts.transpose(0, 1, 3, 2, 4).reshape(LOADS * TILE_STEP, LANES)


def from_tiles(rows):
    parts = rows.reshape(LOADS, XC // 8, TILES, 8, LANES)
    return parts.transpose(0, 1, 3, 2, 4).reshape(LOADS, XC, TILES * LANES)


def tile_row(x, tile):
    return (x // 8) * (8 * TILES) + lax.rem(x, 8) + 8 * tile


def spread_lanes(tile_of, y, lane):
    first = (y * NZ) // LANES
    kind = y % 4
    if kind == 0:
        return tile_of(first)
    if kind == 1:
        return pltpu.roll(jnp.where(lane >= 96, tile_of(first), tile_of(first + 1)), 32, 1)
    if kind == 2:
        return pltpu.roll(jnp.where(lane >= 64, tile_of(first), tile_of(first + 1)), 64, 1)
    return pltpu.roll(tile_of(first), 96, 1)


def pack_lanes(cols, lane):
    one = pltpu.roll(cols[1], 96, 1)
    two = pltpu.roll(cols[2], 64, 1)
    three = pltpu.roll(cols[3], 32, 1)
    return (
        jnp.where(lane < 96, cols[0], one),
        jnp.where(lane < 64, one, two),
        jnp.where(lane < 32, two, three),
    )


def row_of(ref, col, row):
    return jnp.broadcast_to(ref[col, pl.ds(row, 1), :], (LOADS, LANES))


def element_row(low, high, coef):
    v0, w0 = low
    v1, w1 = high
    count = len(v0)
    b0l, b1l, t0l, t1l = [[None] * count for _ in range(4)]

    def add(acc, at, val):
        acc[at] = val if acc[at] is None else acc[at] + val

    for y in range(count - 1):
        even = (v0[y] + w0[y + 1]) + (w1[y] + v1[y + 1])
        odd = (w0[y] + v0[y + 1]) + (v1[y] + w1[y + 1])
        c = coef(y)
        add(b0l, y, c * (even + w1[y + 1]))
        add(b1l, y, c * (odd + v1[y + 1]))
        add(b0l, y + 1, c * (odd + w1[y]))
        add(b1l, y + 1, c * (even + v1[y]))
        add(t0l, y, c * (odd + w0[y + 1]))
        add(t1l, y, c * (even + v0[y + 1]))
        add(t0l, y + 1, c * (even + w0[y]))
        add(t1l, y + 1, c * (odd + v0[y]))
    return (b0l, b1l), (t0l, t1l)


def apply_rows(load_row, coef_at, rows, cols, emit, start):
    def both(i):
        v = load_row(i)
        return v, [pltpu.roll(t, LANES - 1, 1) for t in v]

    inner = range(1, cols - 1)
    low = both(0)
    high = both(1)
    _, top = element_row(low, high, lambda y: coef_at(0, y))

    def body(i, carry):
        v0, w0, t0, t1, extra = carry
        nxt = both(i + 1)
        (b0, b1), (n0, n1) = element_row((v0, w0), nxt, lambda y: coef_at(i, y))
        sums = {
            y: (t0[k] + b0[y]) + pltpu.roll(t1[k] + b1[y], 1, 1) for k, y in enumerate(inner)
        }
        extra = emit(i, sums, extra)
        return nxt[0], nxt[1], [n0[y] for y in inner], [n1[y] for y in inner], extra

    first = (high[0], high[1], [top[0][y] for y in inner], [top[1][y] for y in inner], start)
    return lax.fori_loop(1, rows - 1, body, first)[4]


def kernel(
    gxn, lown, hin, h_hbm, d_hbm, x_out, r_out,
    hv, dd, rv, zv, qv, yv, pv, cu, mi, rows, got0, got1, got2,
    in_sem, heat_send, heat_recv, dens_send, dens_recv, sum_send, sum_recv,
):
    gyn = lown * hin
    ix, iy = lax.axis_index("gx"), lax.axis_index("gy")
    lo, hi = lax.rem(iy, lown), iy // lown
    beside = [
        (lax.rem(ix + dx + gxn, gxn), lax.rem(iy + dy + gyn, gyn)) for dx, dy in SIDES
    ]
    groups = [
        [(ix, hi * lown + lax.rem(lo + r, lown)) for r in range(1, lown)],
        [(ix, lax.rem(hi + r, hin) * lown + lo) for r in range(1, hin)],
        [(lax.rem(ix + r, gxn), iy) for r in range(1, gxn)],
    ]
    partners = beside + groups[0] + groups[1] + groups[2]

    barrier = pltpu.get_barrier_semaphore()
    for one in partners:
        pl.semaphore_signal(barrier, inc=1, device_id=one, device_id_type=MESH)
    take_d = pltpu.make_async_copy(d_hbm, dd.at[pl.ds(8, 16), pl.ds(384, 768)], in_sem.at[1])
    take_h = pltpu.make_async_copy(h_hbm, hv, in_sem.at[0])
    take_h.start()
    take_d.start()
    lane = lax.broadcasted_iota(jnp.int32, (LOADS, LANES), 1)
    sub = lax.broadcasted_iota(jnp.int32, (LOADS, LANES), 0)
    live = lane < NZ
    take_h.wait()

    def lay_out(x, carry):
        tiles = [hv[pl.ds(tile_row(x, t), LOADS, stride=TILE_STEP), :] for t in range(6)]
        for y in range(YC):
            rv[x + 2, y + 2] = jnp.where(live, spread_lanes(lambda t: tiles[t], y, lane), 0.0)
        return carry

    lax.fori_loop(0, XC, lay_out, 0)
    take_d.wait()
    pl.semaphore_wait(barrier, len(partners))

    heat, dens = [], []
    for k, (dx, dy) in enumerate(SIDES):
        copy = pltpu.make_async_remote_copy(
            src_ref=dd.at[pl.ds(*DENS_FROM[dx]), pl.ds(*DENSY_FROM[dy])],
            dst_ref=dd.at[pl.ds(*DENS_TO[dx]), pl.ds(*DENSY_TO[dy])],
            send_sem=dens_send.at[k],
            recv_sem=dens_recv.at[k],
            device_id=beside[k],
            device_id_type=MESH,
        )
        copy.start()
        dens.append(copy)
    for k, (dx, dy) in enumerate(SIDES):
        copy = pltpu.make_async_remote_copy(
            src_ref=rv.at[pl.ds(*HEAT_FROM[dx]), pl.ds(*HEATY_FROM[dy])],
            dst_ref=rv.at[pl.ds(*HEAT_TO[dx]), pl.ds(*HEATY_TO[dy])],
            send_sem=heat_send.at[k],
            recv_sem=heat_recv.at[k],
            device_id=beside[k],
            device_id_type=MESH,
        )
        copy.start()
        heat.append(copy)

    for copy in dens:
        copy.wait_recv()
    for octet in range(4):
        x = sub + (8 * octet - 8)
        x_in = ((x >= 0) | (ix > 0)) & ((x < XC) | (ix < gxn - 1)) & live
        for ey in range(13):
            flat = spread_lanes(
                lambda t, octet=octet: dd[pl.ds(8 * octet, 8), pl.ds(LANES * t, LANES)], ey + 1, lane
            )
            y = ey - 3
            inside = x_in
            if y < 0:
                inside = inside & (iy > 0)
            if y >= YC:
                inside = inside & (iy < gyn - 1)
            c = KMIN + (1.0 - KMIN) * (flat * flat * flat)
            cu[ey, pl.ds(8 * octet, 8), :] = jnp.where(inside, c * (1.0 / 12.0), 0.0)
    lane32 = lax.broadcasted_iota(jnp.int32, (32, LANES), 1)
    x32 = lax.broadcasted_iota(jnp.int32, (32, LANES), 0) - 8
    x_in32 = ((x32 >= 0) | (ix > 0)) & ((x32 < XC) | (ix < gxn - 1)) & (lane32 < NZ)
    for ny in range(YN):
        both = cu[ny] + cu[ny + 1]
        both = both + pltpu.roll(both, 1, 1)
        both = 4.0 * (both + pltpu.roll(both, 1, 0))
        inside = x_in32
        if ny < 2:
            inside = inside & (iy > 0)
        if ny >= YC + 2:
            inside = inside & (iy < gyn - 1)
        mi[ny] = jnp.where(inside, 1.0 / both, 0.0)

    for copy in heat:
        copy.wait_recv()

    def scaled_row(i):
        out = []
        for y in range(YN):
            z = rv[i, y] * row_of(mi, y, i + 6)
            zv[i, y] = z
            out.append(z)
        return out

    def emit_image(i, sums, extra):
        for y, off in sums.items():
            q = 1.25 * rv[i, y] - off
            qv[i - 1, y - 1] = q
            yv[i - 1, y - 1] = q * row_of(mi, y, i + 6)
        return extra

    apply_rows(scaled_row, lambda i, y: row_of(cu, y + 1, i + 6), XN, YN, emit_image, 0)

    def emit_second(i, sums, extra):
        s0, s1, s2, s3 = extra
        for y, off in sums.items():
            q = qv[i, y]
            yy = yv[i, y]
            z = zv[i + 1, y + 1]
            p = 1.25 * q - off
            pv[i - 1, y - 1] = p
            s0 = s0 + rv[i + 1, y + 1] * z
            s1 = s1 + z * q
            s2 = s2 + yy * q
            s3 = s3 + yy * p
        return s0, s1, s2, s3

    zero = jnp.zeros((LOADS, LANES), jnp.float32)
    moments = apply_rows(
        lambda i: [yv[i, y] for y in range(YC + 2)],
        lambda i, y: row_of(cu, y + 2, i + 7),
        XC + 2,
        YC + 2,
        emit_second,
        (zero,) * 4,
    )

    spot = zero
    for k in range(4):
        total = jnp.sum(moments[k], axis=1, keepdims=True)
        spot = spot + jnp.where(lane == 4 * sub + k, total, 0.0)
    rows[0] = jnp.sum(spot, axis=0, keepdims=True)
    sent = []
    done = 0
    for step, (group, got) in enumerate(zip(groups, (got0, got1, got2))):
        copies = []
        for r, one in enumerate(group):
            copies.append(
                pltpu.make_async_remote_copy(
                    src_ref=rows.at[step],
                    dst_ref=got.at[r],
                    send_sem=sum_send.at[done + r],
                    recv_sem=sum_recv.at[done + r],
                    device_id=one,
                    device_id_type=MESH,
                )
            )
        half = len(copies) // 2
        for r in sorted(range(len(copies)), key=lambda r: abs(r - half)):
            copies[r].start()
        for copy in copies:
            copy.wait_recv()
        done += len(copies)
        sent += copies
        total = rows[step]
        for r in range(len(copies)):
            total = total + got[r]
        rows[step + 1] = total

    whole = jnp.broadcast_to(rows[3], (LOADS, LANES))
    s0, s1, s2, s3 = [
        jnp.sum(jnp.where(lane == 4 * sub + k, whole, 0.0), axis=1, keepdims=True) for k in range(4)
    ]
    a0 = s0 / s1
    g = s2 / s1
    mu = (a0 * g - 1.0) / (s3 / s1 - g * g)
    first = jnp.broadcast_to(a0 + mu * g, (LOADS, LANES))
    mu = jnp.broadcast_to(mu, (LOADS, LANES))

    def finish(x, carry):
        for part in range(2):
            xs, rs = [], []
            for k in range(4):
                y = 4 * part + k
                xs.append(first * zv[x + 2, y + 2] - mu * yv[x + 1, y + 1])
                rs.append(rv[x + 2, y + 2] - first * qv[x + 1, y + 1] + mu * pv[x, y])
            for out, cols in ((x_out, xs), (r_out, rs)):
                for t, tile in enumerate(pack_lanes(cols, lane)):
                    out[pl.ds(tile_row(x, 3 * part + t), LOADS, stride=TILE_STEP), :] = tile
        return carry

    lax.fori_loop(0, XC, finish, 0)
    for copy in dens + heat + sent:
        copy.wait_send()


def solution(mesh):
    gxn, gyn = mesh.shape["gx"], mesh.shape["gy"]
    lown = 8 if gyn % 8 == 0 and gyn > 8 else 2
    hin = gyn // lown
    count = (lown - 1) + (hin - 1) + (gxn - 1)

    def per_device(heat_source, density):
        loads, xc, flat = heat_source.shape
        out = jax.ShapeDtypeStruct((loads * xc * flat // LANES, LANES), jnp.float32)
        f32 = jnp.float32
        dma = pltpu.SemaphoreType.DMA
        sol, res = pl.pallas_call(
            functools.partial(kernel, gxn, lown, hin),
            out_shape=(out, out),
            in_specs=[pl.BlockSpec(memory_space=pltpu.HBM)] * 2,
            out_specs=[pl.BlockSpec(memory_space=pltpu.VMEM)] * 2,
            scratch_shapes=[
                pltpu.VMEM((loads * xc * flat // LANES, LANES), f32),
                pltpu.VMEM((32, 1408), f32),
                pltpu.VMEM((XN, YN, LOADS, LANES), f32),
                pltpu.VMEM((XN, YN, LOADS, LANES), f32),
                pltpu.VMEM((XC + 2, YC + 2, LOADS, LANES), f32),
                pltpu.VMEM((XC + 2, YC + 2, LOADS, LANES), f32),
                pltpu.VMEM((XC, YC, LOADS, LANES), f32),
                pltpu.VMEM((13, 32, LANES), f32),
                pltpu.VMEM((YN, 32, LANES), f32),
                pltpu.VMEM((4, 1, LANES), f32),
                pltpu.VMEM((lown - 1, 1, LANES), f32),
                pltpu.VMEM((hin - 1, 1, LANES), f32),
                pltpu.VMEM((gxn - 1, 1, LANES), f32),
                dma((2,)),
                dma((8,)),
                dma((8,)),
                dma((8,)),
                dma((8,)),
                dma((count,)),
                dma((count,)),
            ],
            compiler_params=pltpu.CompilerParams(
                collective_id=0, has_side_effects=True, vmem_limit_bytes=32 * 1024 * 1024
            ),
            name="two_steps",
        )(to_tiles(heat_source), density)
        return from_tiles(sol), from_tiles(res)

    placed = P(None, "gx", "gy")
    return jax.shard_map(
        per_device,
        mesh=mesh,
        in_specs=(placed, P("gx", "gy")),
        out_specs=(placed, placed),
        check_vma=False,
    )
```

```python
import functools

import jax
import jax.numpy as jnp
from jax import lax
from jax.experimental import pallas as pl
from jax.experimental.pallas import tpu as pltpu
from jax.sharding import PartitionSpec as P

NZ = 96
KMIN = 0.001
MESH = pl.DeviceIdType.MESH
LANES = 128
GRANT = 53 * 1024 * 1024
LOADS = 8
XC = 16
YC = 8
XN, YN = XC + 4, YC + 4
SIDES = [(dx, dy) for dx in (-1, 0, 1) for dy in (-1, 0, 1) if (dx, dy) != (0, 0)]

HEAT_FROM = {1: (XC, 2), 0: (2, XC), -1: (2, 2)}
HEAT_TO = {1: (0, 2), 0: (2, XC), -1: (XC + 2, 2)}
HEATY_FROM = {1: (YC, 2), 0: (2, YC), -1: (2, 2)}
HEATY_TO = {1: (0, 2), 0: (2, YC), -1: (YC + 2, 2)}
DENS_FROM = {1: (16, 8), 0: (8, 16), -1: (8, 8)}
DENS_TO = {1: (0, 8), 0: (8, 16), -1: (24, 8)}
DENSY_FROM = {1: (768, 384), 0: (384, 768), -1: (384, 256)}
DENSY_TO = {1: (0, 384), 0: (384, 768), -1: (1152, 256)}


TILES = YC * NZ // LANES
TILE_STEP = XC * TILES


def to_tiles(field):
    parts = field.reshape(LOADS, XC // 8, 8, TILES, LANES)
    return parts.transpose(0, 1, 3, 2, 4).reshape(LOADS * TILE_STEP, LANES)


def from_tiles(rows):
    parts = rows.reshape(LOADS, XC // 8, TILES, 8, LANES)
    return parts.transpose(0, 1, 3, 2, 4).reshape(LOADS, XC, TILES * LANES)


def tile_row(x, tile):
    return (x // 8) * (8 * TILES) + lax.rem(x, 8) + 8 * tile


def spread_lanes(tile_of, y, lane):
    first = (y * NZ) // LANES
    kind = y % 4
    if kind == 0:
        return tile_of(first)
    if kind == 1:
        return pltpu.roll(jnp.where(lane >= 96, tile_of(first), tile_of(first + 1)), 32, 1)
    if kind == 2:
        return pltpu.roll(jnp.where(lane >= 64, tile_of(first), tile_of(first + 1)), 64, 1)
    return pltpu.roll(tile_of(first), 96, 1)


def pack_lanes(cols, lane):
    one = pltpu.roll(cols[1], 96, 1)
    two = pltpu.roll(cols[2], 64, 1)
    three = pltpu.roll(cols[3], 32, 1)
    return (
        jnp.where(lane < 96, cols[0], one),
        jnp.where(lane < 64, one, two),
        jnp.where(lane < 32, two, three),
    )


def row_of(ref, col, row):
    return jnp.broadcast_to(ref[col, pl.ds(row, 1), :], (LOADS, LANES))


def row_fields(tiles):
    ups = [pltpu.roll(t, LANES - 1, 1) for t in tiles]
    s = [t + u for t, u in zip(tiles, ups)]
    d = [t - u for t, u in zip(tiles, ups)]
    return s, d, [s[y] + s[y + 1] for y in range(len(s) - 1)]


def element_row(low, high, coef):
    s0, d0, p0 = low
    s1, d1, p1 = high
    ct, c1, c2, cq, cp = [[] for _ in range(5)]
    for y in range(len(s0) - 1):
        c = coef(y)
        ct.append(c * (p0[y] + p1[y]))
        c1.append(c * (s0[y] - s1[y + 1]))
        c2.append(c * (s0[y + 1] - s1[y]))
        cq.append(c * (d0[y + 1] + d1[y]))
        cp.append(c * (d0[y] + d1[y + 1]))
    inner = range(1, len(s0) - 1)
    u = [ct[y] + ct[y - 1] for y in inner]
    below = (
        [(c1[y] + c2[y - 1]) - u[y - 1] for y in inner],
        [cq[y] + cp[y - 1] for y in inner],
    )
    above = (
        [(c1[y - 1] + c2[y]) + u[y - 1] for y in inner],
        [cq[y - 1] + cp[y] for y in inner],
    )
    return below, above


def apply_rows(load_row, coef_at, rows, emit, start):
    first_row = row_fields(load_row(0))
    second = row_fields(load_row(1))
    _, above = element_row(first_row, second, lambda y: coef_at(0, y))

    def body(i, carry):
        low, (tops, topd), extra = carry
        high = row_fields(load_row(i + 1))
        (bots, botd), above = element_row(low, high, lambda y: coef_at(i, y))
        sums = []
        for k in range(len(bots)):
            n_s = bots[k] - tops[k]
            n_d = botd[k] + topd[k]
            sums.append((n_s + n_d) + pltpu.roll(n_s - n_d, 1, 1))
        return high, above, emit(i, sums, extra)

    return lax.fori_loop(1, rows - 1, body, (second, above, start))[2]


def wrap(i, n):
    return jnp.where(i >= n, i - n, i)


def hops(n):
    known, out = 1, []
    while known < n // 2:
        step = min(known, n // 2 - known)
        out.append(step)
        known += step
    return out


def kernel(
    gxn, lown, hin, h_hbm, d_hbm, x_out, r_out,
    hv, dd, rv, zv, qv, yv, pv, zp, yp, qp, pp, cu, mi, rows, got0, got1, got2,
    in_sem, heat_send, heat_recv, dens_send, dens_recv, sum_send, sum_recv, known,
):
    gyn = lown * hin
    ix, iy = lax.axis_index("gx"), lax.axis_index("gy")
    hi = iy // lown
    lo = iy - hi * lown
    xs_at = {d: wrap(ix + (d + gxn if d < 0 else d), gxn) for d in (-1, 0, 1)}
    ys_at = {d: wrap(iy + (d + gyn if d < 0 else d), gyn) for d in (-1, 0, 1)}
    xs_at[0], ys_at[0] = ix, iy
    beside = [(xs_at[dx], ys_at[dy]) for dx, dy in SIDES]
    groups = [
        [(ix, hi * lown + wrap(lo + r, lown)) for r in range(1, lown)],
        [(ix, wrap(hi + r, hin) * lown + lo) for r in range(1, hin)],
        [(wrap(ix + r, gxn), iy) for r in range(1, gxn)],
    ]
    near = beside + groups[0] + [groups[1][0], groups[1][-1]]

    barrier = pltpu.get_barrier_semaphore()
    for one in near:
        pl.semaphore_signal(barrier, inc=1, device_id=one, device_id_type=MESH)
    turns = []
    for ring, n in ((groups[1], hin), (groups[2], gxn)):
        turns.append([(ring[d - 1], ring[n - 1 - d]) for d in hops(n)])
    count = max(len(t) for t in turns)
    turns = [[t[k] for t in turns if k < len(t)] for k in range(count)]
    flat_turns = [(k, pair) for k, pairs in enumerate(turns) for pair in pairs]

    def tell(k):
        for at, (turn, pair) in enumerate(flat_turns):
            if turn == k:
                for one in pair:
                    pl.semaphore_signal(known.at[at], inc=1, device_id=one, device_id_type=MESH)

    def hear(k):
        for at, (turn, _) in enumerate(flat_turns):
            if turn == k:
                pl.semaphore_wait(known.at[at], 2)

    take_d = pltpu.make_async_copy(d_hbm, dd.at[pl.ds(8, 16), pl.ds(384, 768)], in_sem.at[1])
    take_h = pltpu.make_async_copy(h_hbm, hv, in_sem.at[0])
    take_h.start()
    take_d.start()
    lane = lax.broadcasted_iota(jnp.int32, (LOADS, LANES), 1)
    sub = lax.broadcasted_iota(jnp.int32, (LOADS, LANES), 0)
    live = lane < NZ
    take_h.wait()

    def lay_out(x, carry):
        tiles = [hv[pl.ds(tile_row(x, t), LOADS, stride=TILE_STEP), :] for t in range(6)]
        for y in range(YC):
            rv[x + 2, y + 2] = jnp.where(live, spread_lanes(lambda t: tiles[t], y, lane), 0.0)
        return carry

    lax.fori_loop(0, XC, lay_out, 0)
    take_d.wait()
    pl.semaphore_wait(barrier, len(near))

    heat, dens = [], []
    for k, (dx, dy) in enumerate(SIDES):
        copy = pltpu.make_async_remote_copy(
            src_ref=dd.at[pl.ds(*DENS_FROM[dx]), pl.ds(*DENSY_FROM[dy])],
            dst_ref=dd.at[pl.ds(*DENS_TO[dx]), pl.ds(*DENSY_TO[dy])],
            send_sem=dens_send.at[k],
            recv_sem=dens_recv.at[k],
            device_id=beside[k],
            device_id_type=MESH,
        )
        copy.start()
        dens.append(copy)
    for k, (dx, dy) in enumerate(SIDES):
        copy = pltpu.make_async_remote_copy(
            src_ref=rv.at[pl.ds(*HEAT_FROM[dx]), pl.ds(*HEATY_FROM[dy])],
            dst_ref=rv.at[pl.ds(*HEAT_TO[dx]), pl.ds(*HEATY_TO[dy])],
            send_sem=heat_send.at[k],
            recv_sem=heat_recv.at[k],
            device_id=beside[k],
            device_id_type=MESH,
        )
        copy.start()
        heat.append(copy)

    tell(0)

    for copy in dens:
        copy.wait_recv()
    for k in range(1, count):
        if k == 1:
            hear(0)
            tell(1)
    for octet in range(4):
        x = sub + (8 * octet - 8)
        x_in = ((x >= 0) | (ix > 0)) & ((x < XC) | (ix < gxn - 1)) & live
        for ey in range(13):
            flat = spread_lanes(
                lambda t, octet=octet: dd[pl.ds(8 * octet, 8), pl.ds(LANES * t, LANES)], ey + 1, lane
            )
            y = ey - 3
            inside = x_in
            if y < 0:
                inside = inside & (iy > 0)
            if y >= YC:
                inside = inside & (iy < gyn - 1)
            c = KMIN + (1.0 - KMIN) * (flat * flat * flat)
            cu[ey, pl.ds(8 * octet, 8), :] = jnp.where(inside, c * (1.0 / 24.0), 0.0)
    lane32 = lax.broadcasted_iota(jnp.int32, (32, LANES), 1)
    x32 = lax.broadcasted_iota(jnp.int32, (32, LANES), 0) - 8
    x_in32 = ((x32 >= 0) | (ix > 0)) & ((x32 < XC) | (ix < gxn - 1)) & (lane32 < NZ)
    for ny in range(YN):
        both = cu[ny] + cu[ny + 1]
        both = both + pltpu.roll(both, 1, 1)
        both = 8.0 * (both + pltpu.roll(both, 1, 0))
        inside = x_in32
        if ny < 2:
            inside = inside & (iy > 0)
        if ny >= YC + 2:
            inside = inside & (iy < gyn - 1)
        mi[ny] = jnp.where(inside, 1.0 / both, 0.0)

    zero = jnp.zeros((LOADS, LANES), jnp.float32)

    def first_moment(x, s0):
        for y in range(YC):
            r = rv[x + 2, y + 2]
            s0 = s0 + r * (r * row_of(mi, y + 2, x + 8))
        return s0

    s0 = lax.fori_loop(0, XC, first_moment, zero)
    for copy in heat:
        copy.wait_recv()
    for k in range(1, count - 1):
        hear(k)
        tell(k + 1)

    def scaled_row(i):
        out = []
        for y in range(YN):
            z = rv[i, y] * row_of(mi, y, i + 6)
            zv[i, y] = z
            out.append(z)
        return out

    def emit_image(i, sums, extra):
        for y, off in enumerate(sums):
            q = rv[i, y + 1] + off
            qv[i - 1, y] = q
            yv[i - 1, y] = q * row_of(mi, y + 1, i + 6)
        return extra

    apply_rows(scaled_row, lambda i, y: row_of(cu, y + 1, i + 6), XN, emit_image, 0)

    def emit_second(i, sums, extra):
        s1, s2, s3 = extra
        for y, off in enumerate(sums):
            q = qv[i, y + 1]
            yy = yv[i, y + 1]
            p = q + off
            pv[i - 1, y] = p
            s1 = s1 + zv[i + 1, y + 2] * q
            s2 = s2 + yy * q
            s3 = s3 + yy * p
        return s1, s2, s3

    moments = apply_rows(
        lambda i: [yv[i, y] for y in range(YC + 2)],
        lambda i, y: row_of(cu, y + 2, i + 7),
        XC + 2,
        emit_second,
        (zero,) * 3,
    )
    moments = (s0,) + tuple(moments)
    hear(count - 1)

    spot = zero
    for k in range(4):
        total = jnp.sum(moments[k], axis=1, keepdims=True)
        spot = spot + jnp.where(lane == 4 * sub + k, total, 0.0)
    rows[0] = jnp.sum(spot, axis=0, keepdims=True)
    def pack(x, carry):
        for ref, out, dx, dy in ((zv, zp, 2, 2), (yv, yp, 1, 1), (qv, qp, 1, 1), (pv, pp, 0, 0)):
            for part in range(2):
                cols = [ref[x + dx, 4 * part + k + dy] for k in range(4)]
                for t, tile in enumerate(pack_lanes(cols, lane)):
                    out[pl.ds(tile_row(x, 3 * part + t), LOADS, stride=TILE_STEP), :] = tile
        return carry

    sent = []
    done = 0
    for step, (group, got) in enumerate(zip(groups, (got0, got1, got2))):
        copies = []
        for r, one in enumerate(group):
            copies.append(
                pltpu.make_async_remote_copy(
                    src_ref=rows.at[step],
                    dst_ref=got.at[r],
                    send_sem=sum_send.at[done + r],
                    recv_sem=sum_recv.at[done + r],
                    device_id=one,
                    device_id_type=MESH,
                )
            )
        half = len(copies) // 2
        for r in sorted(range(len(copies)), key=lambda r: abs(r - half)):
            copies[r].start()
        if step == len(groups) - 1:
            lax.fori_loop(0, XC, pack, 0)
        for copy in copies:
            copy.wait_recv()
        done += len(copies)
        sent += copies
        total = rows[step]
        for r in range(len(copies)):
            total = total + got[r]
        rows[step + 1] = total

    whole = jnp.broadcast_to(rows[3], (LOADS, LANES))
    s0, s1, s2, s3 = [
        jnp.sum(jnp.where(lane == 4 * sub + k, whole, 0.0), axis=1, keepdims=True) for k in range(4)
    ]
    a0 = s0 / s1
    g = s2 / s1
    mu = (a0 * g - 1.0) / (s3 / s1 - g * g)
    first = a0 + mu * g
    for load in range(LOADS):
        f = jnp.broadcast_to(first[load : load + 1], (LOADS, LANES))
        m = jnp.broadcast_to(mu[load : load + 1], (LOADS, LANES))
        for t in range(TILE_STEP // 8):
            at = pl.ds(load * TILE_STEP + 8 * t, 8)
            x_out[at, :] = f * zp[at, :] - m * yp[at, :]
            r_out[at, :] = (hv[at, :] - f * qp[at, :]) + m * pp[at, :]
    for copy in dens + heat + sent:
        copy.wait_send()


def put_out(x, r, x_out, r_out, sem):
    copies = [pltpu.make_async_copy(x, x_out, sem.at[0]), pltpu.make_async_copy(r, r_out, sem.at[1])]
    for copy in copies:
        copy.start()
    for copy in copies:
        copy.wait()


def solution(mesh):
    gxn, gyn = mesh.shape["gx"], mesh.shape["gy"]
    lown = 8 if gyn % 8 == 0 and gyn > 8 else 2
    hin = gyn // lown
    count = (lown - 1) + (hin - 1) + (gxn - 1)

    def per_device(heat_source, density):
        loads, xc, flat = heat_source.shape
        out = jax.ShapeDtypeStruct((loads * xc * flat // LANES, LANES), jnp.float32)
        f32 = jnp.float32
        dma = pltpu.SemaphoreType.DMA
        sol, res = pl.pallas_call(
            functools.partial(kernel, gxn, lown, hin),
            out_shape=(out, out),
            in_specs=[pl.BlockSpec(memory_space=pltpu.HBM)] * 2,
            out_specs=[pl.BlockSpec(memory_space=pltpu.VMEM)] * 2,
            scratch_shapes=[
                pltpu.VMEM((LOADS * TILE_STEP, LANES), f32),
                pltpu.VMEM((32, 1408), f32),
                pltpu.VMEM((XN, YN, LOADS, LANES), f32),
                pltpu.VMEM((XN, YN, LOADS, LANES), f32),
                pltpu.VMEM((XC + 2, YC + 2, LOADS, LANES), f32),
                pltpu.VMEM((XC + 2, YC + 2, LOADS, LANES), f32),
                pltpu.VMEM((XC, YC, LOADS, LANES), f32),
                pltpu.VMEM((LOADS * TILE_STEP, LANES), f32),
                pltpu.VMEM((LOADS * TILE_STEP, LANES), f32),
                pltpu.VMEM((LOADS * TILE_STEP, LANES), f32),
                pltpu.VMEM((LOADS * TILE_STEP, LANES), f32),
                pltpu.VMEM((13, 32, LANES), f32),
                pltpu.VMEM((YN, 32, LANES), f32),
                pltpu.VMEM((4, 1, LANES), f32),
                pltpu.VMEM((lown - 1, 1, LANES), f32),
                pltpu.VMEM((hin - 1, 1, LANES), f32),
                pltpu.VMEM((gxn - 1, 1, LANES), f32),
                dma((2,)),
                dma((8,)),
                dma((8,)),
                dma((8,)),
                dma((8,)),
                dma((count,)),
                dma((count,)),
                pltpu.SemaphoreType.REGULAR((len(hops(hin)) + len(hops(gxn)),)),
            ],
            compiler_params=pltpu.CompilerParams(
                collective_id=0, has_side_effects=True, vmem_limit_bytes=GRANT
            ),
            name="two_steps",
        )(to_tiles(heat_source), density)
        sol, res = pl.pallas_call(
            put_out,
            out_shape=(out, out),
            in_specs=[pl.BlockSpec(memory_space=pltpu.VMEM)] * 2,
            out_specs=[pl.BlockSpec(memory_space=pltpu.HBM)] * 2,
            scratch_shapes=[dma((2,))],
            compiler_params=pltpu.CompilerParams(vmem_limit_bytes=2 * 1024 * 1024),
            name="put_out",
        )(sol, res)
        return from_tiles(sol), from_tiles(res)

    placed = P(None, "gx", "gy")
    return jax.shard_map(
        per_device,
        mesh=mesh,
        in_specs=(placed, P("gx", "gy")),
        out_specs=(placed, placed),
        check_vma=False,
    )
```

```python
import functools
import math

import jax
import jax.numpy as jnp
from jax import lax
from jax.experimental import pallas as pl
from jax.experimental.pallas import tpu as pltpu
from jax.sharding import PartitionSpec as P

NZ = 96
KMIN = 0.001
MESH = pl.DeviceIdType.MESH
LANES = 128
GRANT = 53 * 1024 * 1024
BY_IMAGE, BY_SECOND = 6, 8
LOADS = 8
XC = 16
YC = 8
XN, YN = XC + 4, YC + 4
SIDES = [(dx, dy) for dx in (-1, 0, 1) for dy in (-1, 0, 1) if (dx, dy) != (0, 0)]

HEAT_FROM = {1: (XC, 2), 0: (2, XC), -1: (2, 2)}
HEAT_TO = {1: (0, 2), 0: (2, XC), -1: (XC + 2, 2)}
HEATY_FROM = {1: (YC, 2), 0: (2, YC), -1: (2, 2)}
HEATY_TO = {1: (0, 2), 0: (2, YC), -1: (YC + 2, 2)}
DENS_FROM = {1: (16, 8), 0: (8, 16), -1: (8, 8)}
DENS_TO = {1: (0, 8), 0: (8, 16), -1: (24, 8)}
DENSY_FROM = {1: (768, 384), 0: (384, 768), -1: (384, 256)}
DENSY_TO = {1: (0, 384), 0: (384, 768), -1: (1152, 256)}


TILES = YC * NZ // LANES
TILE_STEP = XC * TILES


def to_tiles(field):
    parts = field.reshape(LOADS, XC // 8, 8, TILES, LANES)
    return parts.transpose(0, 1, 3, 2, 4).reshape(LOADS * TILE_STEP, LANES)


def from_tiles(rows):
    parts = rows.reshape(LOADS, XC // 8, TILES, 8, LANES)
    return parts.transpose(0, 1, 3, 2, 4).reshape(LOADS, XC, TILES * LANES)


def tile_row(x, tile):
    return (x // 8) * (8 * TILES) + lax.rem(x, 8) + 8 * tile


def spread_lanes(tile_of, y, lane):
    first = (y * NZ) // LANES
    kind = y % 4
    if kind == 0:
        return tile_of(first)
    if kind == 1:
        return pltpu.roll(jnp.where(lane >= 96, tile_of(first), tile_of(first + 1)), 32, 1)
    if kind == 2:
        return pltpu.roll(jnp.where(lane >= 64, tile_of(first), tile_of(first + 1)), 64, 1)
    return pltpu.roll(tile_of(first), 96, 1)


def pack_lanes(cols, lane):
    one = pltpu.roll(cols[1], 96, 1)
    two = pltpu.roll(cols[2], 64, 1)
    three = pltpu.roll(cols[3], 32, 1)
    return (
        jnp.where(lane < 96, cols[0], one),
        jnp.where(lane < 64, one, two),
        jnp.where(lane < 32, two, three),
    )


def row_of(ref, col, row):
    return jnp.broadcast_to(ref[col, pl.ds(row, 1), :], (LOADS, LANES))


def row_fields(tiles):
    ups = [pltpu.roll(t, LANES - 1, 1) for t in tiles]
    s = [t + u for t, u in zip(tiles, ups)]
    d = [t - u for t, u in zip(tiles, ups)]
    return s, d, [s[y] + s[y + 1] for y in range(len(s) - 1)]


def element_row(low, high, coef):
    s0, d0, p0 = low
    s1, d1, p1 = high
    ct, c1, c2, cq, cp = [[] for _ in range(5)]
    for y in range(len(s0) - 1):
        c = coef(y)
        ct.append(c * (p0[y] + p1[y]))
        c1.append(c * (s0[y] - s1[y + 1]))
        c2.append(c * (s0[y + 1] - s1[y]))
        cq.append(c * (d0[y + 1] + d1[y]))
        cp.append(c * (d0[y] + d1[y + 1]))
    inner = range(1, len(s0) - 1)
    u = [ct[y] + ct[y - 1] for y in inner]
    below = (
        [(c1[y] + c2[y - 1]) - u[y - 1] for y in inner],
        [cq[y] + cp[y - 1] for y in inner],
    )
    above = (
        [(c1[y - 1] + c2[y]) + u[y - 1] for y in inner],
        [cq[y - 1] + cp[y] for y in inner],
    )
    return below, above


def apply_rows(load_row, coef_at, rows, emit, start, by):
    first_row = row_fields(load_row(0))
    second = row_fields(load_row(1))
    _, above = element_row(first_row, second, lambda y: coef_at(0, y))

    def body(i, carry):
        low, (tops, topd), extra = carry
        high = row_fields(load_row(i + 1))
        (bots, botd), above = element_row(low, high, lambda y: coef_at(i, y))
        sums = []
        for k in range(len(bots)):
            n_s = bots[k] - tops[k]
            n_d = botd[k] + topd[k]
            sums.append((n_s + n_d) + pltpu.roll(n_s - n_d, 1, 1))
        return high, above, emit(i, sums, extra)

    return walk(1, rows - 1, body, (second, above, start), by)[2]


def walk(start, stop, body, carry, by):
    def turn(t, carry):
        for k in range(by):
            carry = body(start + t * by + k, carry)
        return carry

    turns = (stop - start) // by
    if turns == 1:
        for k in range(by):
            carry = body(start + k, carry)
        return carry
    return lax.fori_loop(0, turns, turn, carry)


def wrap(i, n):
    return jnp.where(i >= n, i - n, i)


def hops(n, known):
    ahead, out = 1 - known, []
    while known < n // 2:
        step = min(known + ahead, n // 2 - known)
        out.append(step)
        known += step
    return out


def turns_of(xn, yn, zn):
    return [(1, 1, zn, 2), (xn, yn, 1, 1)]


def kernel(
    gxn, lown, hin, h_hbm, d_hbm, x_out, r_out,
    hv, dd, rv, zv, qv, yv, pv, zp, yp, qp, pp, cu, mi, rows, got,
    in_sem, heat_send, heat_recv, dens_send, dens_recv, sum_send, sum_recv, known,
):
    gyn = lown * hin
    ix, iy = lax.axis_index("gx"), lax.axis_index("gy")
    hi = iy // lown
    lo = iy - hi * lown
    xs_at = {d: wrap(ix + (d + gxn if d < 0 else d), gxn) for d in (-1, 0, 1)}
    ys_at = {d: wrap(iy + (d + gyn if d < 0 else d), gyn) for d in (-1, 0, 1)}
    xs_at[0], ys_at[0] = ix, iy
    beside = [(xs_at[dx], ys_at[dy]) for dx, dy in SIDES]
    rings = [
        [(ix, hi * lown + wrap(lo + r, lown)) for r in range(1, lown)],
        [(ix, wrap(hi + r, hin) * lown + lo) for r in range(1, hin)],
        [(wrap(ix + r, gxn), iy) for r in range(1, gxn)],
    ]
    core = lo - 2 * (lo // 2)
    groups = []
    for xs, ys, zs, cores in turns_of(lown // 2, hin, gxn):
        group = []
        for dx in range(xs):
            for dy in range(ys):
                for dz in range(zs):
                    for dc in range(cores):
                        far = sum(min(d, n - d) for d, n in ((dx, xs), (dy, ys), (dz, zs)))
                        if far + dc == 0:
                            continue
                        at = wrap(lo + 2 * dx, lown)
                        if dc:
                            at = at + 1 - 2 * core
                        group.append((-far, (wrap(ix + dz, gxn), wrap(hi + dy, hin) * lown + at)))
        groups.append([one for _, one in sorted(group, key=lambda g: g[0])])
    near = beside + rings[0] + [rings[1][0], rings[1][-1]]

    barrier = pltpu.get_barrier_semaphore()
    for one in near:
        pl.semaphore_signal(barrier, inc=1, device_id=one, device_id_type=MESH)
    turns = []
    for ring, n, known_at in ((rings[1], hin, 0), (rings[2], gxn, 1)):
        turns.append([(ring[d - 1], ring[n - 1 - d]) for d in hops(n, known_at)])
    count = max(len(t) for t in turns)
    turns = [[t[k] for t in turns if k < len(t)] for k in range(count)]
    flat_turns = [(k, pair) for k, pairs in enumerate(turns) for pair in pairs]

    def tell(k):
        for at, (turn, pair) in enumerate(flat_turns):
            if turn == k:
                for one in pair:
                    pl.semaphore_signal(known.at[at], inc=1, device_id=one, device_id_type=MESH)

    def hear(k):
        for at, (turn, _) in enumerate(flat_turns):
            if turn == k:
                pl.semaphore_wait(known.at[at], 2)

    take_d = pltpu.make_async_copy(d_hbm, dd.at[pl.ds(8, 16), pl.ds(384, 768)], in_sem.at[1])
    take_h = pltpu.make_async_copy(h_hbm, hv, in_sem.at[0])
    take_h.start()
    take_d.start()
    lane = lax.broadcasted_iota(jnp.int32, (LOADS, LANES), 1)
    sub = lax.broadcasted_iota(jnp.int32, (LOADS, LANES), 0)
    live = lane < NZ
    take_h.wait()

    def lay_out(x, carry):
        tiles = [hv[pl.ds(tile_row(x, t), LOADS, stride=TILE_STEP), :] for t in range(6)]
        for y in range(YC):
            rv[x + 2, y + 2] = jnp.where(live, spread_lanes(lambda t: tiles[t], y, lane), 0.0)
        return carry

    walk(0, XC, lay_out, 0, 4)
    take_d.wait()
    pl.semaphore_wait(barrier, len(near))

    heat, dens = [], []
    for k, (dx, dy) in enumerate(SIDES):
        copy = pltpu.make_async_remote_copy(
            src_ref=dd.at[pl.ds(*DENS_FROM[dx]), pl.ds(*DENSY_FROM[dy])],
            dst_ref=dd.at[pl.ds(*DENS_TO[dx]), pl.ds(*DENSY_TO[dy])],
            send_sem=dens_send.at[k],
            recv_sem=dens_recv.at[k],
            device_id=beside[k],
            device_id_type=MESH,
        )
        copy.start()
        dens.append(copy)
    for k, (dx, dy) in enumerate(SIDES):
        copy = pltpu.make_async_remote_copy(
            src_ref=rv.at[pl.ds(*HEAT_FROM[dx]), pl.ds(*HEATY_FROM[dy])],
            dst_ref=rv.at[pl.ds(*HEAT_TO[dx]), pl.ds(*HEATY_TO[dy])],
            send_sem=heat_send.at[k],
            recv_sem=heat_recv.at[k],
            device_id=beside[k],
            device_id_type=MESH,
        )
        copy.start()
        heat.append(copy)

    tell(0)

    for copy in dens:
        copy.wait_recv()
    for k in range(1, count):
        if k == 1:
            hear(0)
            tell(1)
    for octet in range(4):
        x = sub + (8 * octet - 8)
        x_in = ((x >= 0) | (ix > 0)) & ((x < XC) | (ix < gxn - 1)) & live
        for ey in range(13):
            flat = spread_lanes(
                lambda t, octet=octet: dd[pl.ds(8 * octet, 8), pl.ds(LANES * t, LANES)], ey + 1, lane
            )
            y = ey - 3
            inside = x_in
            if y < 0:
                inside = inside & (iy > 0)
            if y >= YC:
                inside = inside & (iy < gyn - 1)
            c = KMIN + (1.0 - KMIN) * (flat * flat * flat)
            cu[ey, pl.ds(8 * octet, 8), :] = jnp.where(inside, c * (1.0 / 24.0), 0.0)
    lane32 = lax.broadcasted_iota(jnp.int32, (32, LANES), 1)
    x32 = lax.broadcasted_iota(jnp.int32, (32, LANES), 0) - 8
    x_in32 = ((x32 >= 0) | (ix > 0)) & ((x32 < XC) | (ix < gxn - 1)) & (lane32 < NZ)
    for ny in range(YN):
        both = cu[ny] + cu[ny + 1]
        both = both + pltpu.roll(both, 1, 1)
        both = 8.0 * (both + pltpu.roll(both, 1, 0))
        inside = x_in32
        if ny < 2:
            inside = inside & (iy > 0)
        if ny >= YC + 2:
            inside = inside & (iy < gyn - 1)
        mi[ny] = jnp.where(inside, 1.0 / both, 0.0)

    zero = jnp.zeros((LOADS, LANES), jnp.float32)

    def first_moment(x, s0):
        for y in range(YC):
            r = rv[x + 2, y + 2]
            s0 = s0 + r * (r * row_of(mi, y + 2, x + 8))
        return s0

    s0 = walk(0, XC, first_moment, zero, 2)
    for copy in heat:
        copy.wait_recv()
    for k in range(1, count - 1):
        hear(k)
        tell(k + 1)

    def scaled_row(i):
        out = []
        for y in range(YN):
            z = rv[i, y] * row_of(mi, y, i + 6)
            zv[i, y] = z
            out.append(z)
        return out

    def emit_image(i, sums, extra):
        for y, off in enumerate(sums):
            q = rv[i, y + 1] + off
            qv[i - 1, y] = q
            yv[i - 1, y] = q * row_of(mi, y + 1, i + 6)
        return extra

    apply_rows(scaled_row, lambda i, y: row_of(cu, y + 1, i + 6), XN, emit_image, 0, BY_IMAGE)

    def emit_second(i, sums, extra):
        s1, s2, s3 = extra
        for y, off in enumerate(sums):
            q = qv[i, y + 1]
            yy = yv[i, y + 1]
            p = q + off
            pv[i - 1, y] = p
            s1 = s1 + zv[i + 1, y + 2] * q
            s2 = s2 + yy * q
            s3 = s3 + yy * p
        return s1, s2, s3

    moments = apply_rows(
        lambda i: [yv[i, y] for y in range(YC + 2)],
        lambda i, y: row_of(cu, y + 2, i + 7),
        XC + 2,
        emit_second,
        (zero,) * 3,
        BY_SECOND,
    )
    moments = (s0,) + tuple(moments)
    hear(count - 1)

    spot = zero
    for k in range(4):
        total = jnp.sum(moments[k], axis=1, keepdims=True)
        spot = spot + jnp.where(lane == 4 * sub + k, total, 0.0)
    rows[0] = jnp.sum(spot, axis=0, keepdims=True)
    def pack(x, carry):
        for ref, out, dx, dy in ((zv, zp, 2, 2), (yv, yp, 1, 1), (qv, qp, 1, 1), (pv, pp, 0, 0)):
            for part in range(2):
                cols = [ref[x + dx, 4 * part + k + dy] for k in range(4)]
                for t, tile in enumerate(pack_lanes(cols, lane)):
                    out[pl.ds(tile_row(x, 3 * part + t), LOADS, stride=TILE_STEP), :] = tile
        return carry

    sent = []
    done = 0
    for step, group in enumerate(groups):
        copies = []
        for r, one in enumerate(group):
            copies.append(
                pltpu.make_async_remote_copy(
                    src_ref=rows.at[step],
                    dst_ref=got.at[done + r],
                    send_sem=sum_send.at[done + r],
                    recv_sem=sum_recv.at[done + r],
                    device_id=one,
                    device_id_type=MESH,
                )
            )
        for copy in copies:
            copy.start()
        if step == len(groups) - 1:
            walk(0, XC, pack, 0, 2)
        for copy in copies:
            copy.wait_recv()
        total = rows[step]
        for r in range(len(copies)):
            total = total + got[done + r]
        rows[step + 1] = total
        done += len(copies)
        sent += copies

    whole = jnp.broadcast_to(rows[len(groups)], (LOADS, LANES))
    s0, s1, s2, s3 = [
        jnp.sum(jnp.where(lane == 4 * sub + k, whole, 0.0), axis=1, keepdims=True) for k in range(4)
    ]
    a0 = s0 / s1
    g = s2 / s1
    mu = (a0 * g - 1.0) / (s3 / s1 - g * g)
    first = a0 + mu * g
    for load in range(LOADS):
        f = jnp.broadcast_to(first[load : load + 1], (LOADS, LANES))
        m = jnp.broadcast_to(mu[load : load + 1], (LOADS, LANES))
        for t in range(TILE_STEP // 8):
            at = pl.ds(load * TILE_STEP + 8 * t, 8)
            x_out[at, :] = f * zp[at, :] - m * yp[at, :]
            r_out[at, :] = (hv[at, :] - f * qp[at, :]) + m * pp[at, :]
    for copy in dens + heat + sent:
        copy.wait_send()


def put_out(x, r, x_out, r_out, sem):
    copies = [pltpu.make_async_copy(x, x_out, sem.at[0]), pltpu.make_async_copy(r, r_out, sem.at[1])]
    for copy in copies:
        copy.start()
    for copy in copies:
        copy.wait()


def solution(mesh):
    gxn, gyn = mesh.shape["gx"], mesh.shape["gy"]
    lown = 8 if gyn % 8 == 0 and gyn > 8 else 2
    hin = gyn // lown
    count = sum(math.prod(t) - 1 for t in turns_of(lown // 2, hin, gxn))

    def per_device(heat_source, density):
        loads, xc, flat = heat_source.shape
        out = jax.ShapeDtypeStruct((loads * xc * flat // LANES, LANES), jnp.float32)
        f32 = jnp.float32
        dma = pltpu.SemaphoreType.DMA
        sol, res = pl.pallas_call(
            functools.partial(kernel, gxn, lown, hin),
            out_shape=(out, out),
            in_specs=[pl.BlockSpec(memory_space=pltpu.HBM)] * 2,
            out_specs=[pl.BlockSpec(memory_space=pltpu.VMEM)] * 2,
            scratch_shapes=[
                pltpu.VMEM((LOADS * TILE_STEP, LANES), f32),
                pltpu.VMEM((32, 1408), f32),
                pltpu.VMEM((XN, YN, LOADS, LANES), f32),
                pltpu.VMEM((XN, YN, LOADS, LANES), f32),
                pltpu.VMEM((XC + 2, YC + 2, LOADS, LANES), f32),
                pltpu.VMEM((XC + 2, YC + 2, LOADS, LANES), f32),
                pltpu.VMEM((XC, YC, LOADS, LANES), f32),
                pltpu.VMEM((LOADS * TILE_STEP, LANES), f32),
                pltpu.VMEM((LOADS * TILE_STEP, LANES), f32),
                pltpu.VMEM((LOADS * TILE_STEP, LANES), f32),
                pltpu.VMEM((LOADS * TILE_STEP, LANES), f32),
                pltpu.VMEM((13, 32, LANES), f32),
                pltpu.VMEM((YN, 32, LANES), f32),
                pltpu.VMEM((4, 1, LANES), f32),
                pltpu.VMEM((count, 1, LANES), f32),
                dma((2,)),
                dma((8,)),
                dma((8,)),
                dma((8,)),
                dma((8,)),
                dma((count,)),
                dma((count,)),
                pltpu.SemaphoreType.REGULAR((len(hops(hin, 0)) + len(hops(gxn, 1)),)),
            ],
            compiler_params=pltpu.CompilerParams(
                collective_id=0, has_side_effects=True, vmem_limit_bytes=GRANT
            ),
            name="two_steps",
        )(to_tiles(heat_source), density)
        sol, res = pl.pallas_call(
            put_out,
            out_shape=(out, out),
            in_specs=[pl.BlockSpec(memory_space=pltpu.VMEM)] * 2,
            out_specs=[pl.BlockSpec(memory_space=pltpu.HBM)] * 2,
            scratch_shapes=[dma((2,))],
            compiler_params=pltpu.CompilerParams(vmem_limit_bytes=2 * 1024 * 1024),
            name="put_out",
        )(sol, res)
        return from_tiles(sol), from_tiles(res)

    placed = P(None, "gx", "gy")
    return jax.shard_map(
        per_device,
        mesh=mesh,
        in_specs=(placed, P("gx", "gy")),
        out_specs=(placed, placed),
        check_vma=False,
    )
```

```python
import functools
import math

import jax
import jax.numpy as jnp
from jax import lax
from jax.experimental import pallas as pl
from jax.experimental.pallas import tpu as pltpu
from jax.sharding import PartitionSpec as P

NZ = 96
KMIN = 0.001
MESH = pl.DeviceIdType.MESH
LANES = 128
GRANT = 53 * 1024 * 1024
BY_IMAGE, BY_SECOND = 6, 8
LOADS = 8
XC = 16
YC = 8
XN, YN = XC + 4, YC + 4
SIDES = [(dx, dy) for dx in (-1, 0, 1) for dy in (-1, 0, 1) if (dx, dy) != (0, 0)]

HEAT_FROM = {1: (XC, 2), 0: (2, XC), -1: (2, 2)}
HEAT_TO = {1: (0, 2), 0: (2, XC), -1: (XC + 2, 2)}
HEATY_FROM = {1: (YC, 2), 0: (2, YC), -1: (2, 2)}
HEATY_TO = {1: (0, 2), 0: (2, YC), -1: (YC + 2, 2)}
DENS_FROM = {1: (16, 8), 0: (8, 16), -1: (8, 8)}
DENS_TO = {1: (0, 8), 0: (8, 16), -1: (24, 8)}
DENSY_FROM = {1: (768, 384), 0: (384, 768), -1: (384, 256)}
DENSY_TO = {1: (0, 384), 0: (384, 768), -1: (1152, 256)}


TILES = YC * NZ // LANES
TILE_STEP = XC * TILES


def to_tiles(field):
    parts = field.reshape(LOADS, XC // 8, 8, TILES, LANES)
    return parts.transpose(0, 1, 3, 2, 4).reshape(LOADS * TILE_STEP, LANES)


def from_tiles(rows):
    parts = rows.reshape(LOADS, XC // 8, TILES, 8, LANES)
    return parts.transpose(0, 1, 3, 2, 4).reshape(LOADS, XC, TILES * LANES)


def tile_row(x, tile):
    return (x // 8) * (8 * TILES) + lax.rem(x, 8) + 8 * tile


def spread_lanes(tile_of, y, lane):
    first = (y * NZ) // LANES
    kind = y % 4
    if kind == 0:
        return tile_of(first)
    if kind == 1:
        return pltpu.roll(jnp.where(lane >= 96, tile_of(first), tile_of(first + 1)), 32, 1)
    if kind == 2:
        return pltpu.roll(jnp.where(lane >= 64, tile_of(first), tile_of(first + 1)), 64, 1)
    return pltpu.roll(tile_of(first), 96, 1)


def pack_lanes(cols, lane):
    one = pltpu.roll(cols[1], 96, 1)
    two = pltpu.roll(cols[2], 64, 1)
    three = pltpu.roll(cols[3], 32, 1)
    return (
        jnp.where(lane < 96, cols[0], one),
        jnp.where(lane < 64, one, two),
        jnp.where(lane < 32, two, three),
    )


def row_of(ref, col, row):
    return jnp.broadcast_to(ref[col, pl.ds(row, 1), :], (LOADS, LANES))


def row_fields(tiles):
    ups = [pltpu.roll(t, LANES - 1, 1) for t in tiles]
    s = [t + u for t, u in zip(tiles, ups)]
    d = [t - u for t, u in zip(tiles, ups)]
    return s, d, [s[y] + s[y + 1] for y in range(len(s) - 1)]


def element_row(low, high, coef):
    s0, d0, p0 = low
    s1, d1, p1 = high
    ct, c1, c2, cq, cp = [[] for _ in range(5)]
    for y in range(len(s0) - 1):
        c = coef(y)
        ct.append(c * (p0[y] + p1[y]))
        c1.append(c * (s0[y] - s1[y + 1]))
        c2.append(c * (s0[y + 1] - s1[y]))
        cq.append(c * (d0[y + 1] + d1[y]))
        cp.append(c * (d0[y] + d1[y + 1]))
    inner = range(1, len(s0) - 1)
    u = [ct[y] + ct[y - 1] for y in inner]
    below = (
        [(c1[y] + c2[y - 1]) - u[y - 1] for y in inner],
        [cq[y] + cp[y - 1] for y in inner],
    )
    above = (
        [(c1[y - 1] + c2[y]) + u[y - 1] for y in inner],
        [cq[y - 1] + cp[y] for y in inner],
    )
    return below, above


def apply_rows(load_row, coef_at, rows, emit, start, by):
    first_row = row_fields(load_row(0))
    second = row_fields(load_row(1))
    _, above = element_row(first_row, second, lambda y: coef_at(0, y))

    def body(i, carry):
        low, (tops, topd), extra = carry
        high = row_fields(load_row(i + 1))
        (bots, botd), above = element_row(low, high, lambda y: coef_at(i, y))
        sums = []
        for k in range(len(bots)):
            n_s = bots[k] - tops[k]
            n_d = botd[k] + topd[k]
            sums.append((n_s + n_d) + pltpu.roll(n_s - n_d, 1, 1))
        return high, above, emit(i, sums, extra)

    return walk(1, rows - 1, body, (second, above, start), by)[2]


def walk(start, stop, body, carry, by):
    def turn(t, carry):
        for k in range(by):
            carry = body(start + t * by + k, carry)
        return carry

    turns = (stop - start) // by
    if turns == 1:
        for k in range(by):
            carry = body(start + k, carry)
        return carry
    return lax.fori_loop(0, turns, turn, carry)


def tree(terms):
    while len(terms) > 1:
        pairs = [terms[k] + terms[k + 1] for k in range(0, len(terms) - 1, 2)]
        terms = pairs + terms[len(terms) - len(terms) % 2 :]
    return terms[0]


def wrap(i, n):
    return jnp.where(i >= n, i - n, i)


def hops(n, known):
    ahead, out = 1 - known, []
    while known < n // 2:
        step = min(known + ahead, n // 2 - known)
        out.append(step)
        known += step
    return out


def turns_of(xn, yn, zn):
    return [(1, 1, zn, 2), (xn, yn, 1, 1)]


def kernel(
    gxn, lown, hin, h_hbm, d_hbm, x_out, r_out,
    hv, dd, rv, zv, qv, yv, pv, zp, yp, qp, pp, cu, mi, rows, got,
    in_sem, heat_send, heat_recv, dens_send, dens_recv, sum_send, sum_recv, known,
):
    gyn = lown * hin
    ix, iy = lax.axis_index("gx"), lax.axis_index("gy")
    hi = iy // lown
    lo = iy - hi * lown
    xs_at = {d: wrap(ix + (d + gxn if d < 0 else d), gxn) for d in (-1, 0, 1)}
    ys_at = {d: wrap(iy + (d + gyn if d < 0 else d), gyn) for d in (-1, 0, 1)}
    xs_at[0], ys_at[0] = ix, iy
    beside = [(xs_at[dx], ys_at[dy]) for dx, dy in SIDES]
    rings = [
        [(ix, hi * lown + wrap(lo + r, lown)) for r in range(1, lown)],
        [(ix, wrap(hi + r, hin) * lown + lo) for r in range(1, hin)],
        [(wrap(ix + r, gxn), iy) for r in range(1, gxn)],
    ]
    core = lo - 2 * (lo // 2)
    groups = []
    for xs, ys, zs, cores in turns_of(lown // 2, hin, gxn):
        group = []
        for dx in range(xs):
            for dy in range(ys):
                for dz in range(zs):
                    for dc in range(cores):
                        far = sum(min(d, n - d) for d, n in ((dx, xs), (dy, ys), (dz, zs)))
                        if far + dc == 0:
                            continue
                        at = wrap(lo + 2 * dx, lown)
                        if dc:
                            at = at + 1 - 2 * core
                        group.append((-far, (wrap(ix + dz, gxn), wrap(hi + dy, hin) * lown + at)))
        groups.append([one for _, one in sorted(group, key=lambda g: g[0])])
    near = beside + rings[0] + [rings[1][0], rings[1][-1]]

    barrier = pltpu.get_barrier_semaphore()
    for one in near:
        pl.semaphore_signal(barrier, inc=1, device_id=one, device_id_type=MESH)
    turns = []
    for ring, n, known_at in ((rings[1], hin, 0), (rings[2], gxn, 1)):
        turns.append([(ring[d - 1], ring[n - 1 - d]) for d in hops(n, known_at)])
    count = max(len(t) for t in turns)
    turns = [[t[k] for t in turns if k < len(t)] for k in range(count)]
    flat_turns = [(k, pair) for k, pairs in enumerate(turns) for pair in pairs]

    def tell(k):
        for at, (turn, pair) in enumerate(flat_turns):
            if turn == k:
                for one in pair:
                    pl.semaphore_signal(known.at[at], inc=1, device_id=one, device_id_type=MESH)

    def hear(k):
        for at, (turn, _) in enumerate(flat_turns):
            if turn == k:
                pl.semaphore_wait(known.at[at], 2)

    take_d = pltpu.make_async_copy(d_hbm, dd.at[pl.ds(8, 16), pl.ds(384, 768)], in_sem.at[1])
    take_h = pltpu.make_async_copy(h_hbm, hv, in_sem.at[0])
    take_h.start()
    take_d.start()
    lane = lax.broadcasted_iota(jnp.int32, (LOADS, LANES), 1)
    sub = lax.broadcasted_iota(jnp.int32, (LOADS, LANES), 0)
    live = lane < NZ
    take_h.wait()

    def lay_out(x, carry):
        tiles = [hv[pl.ds(tile_row(x, t), LOADS, stride=TILE_STEP), :] for t in range(6)]
        for y in range(YC):
            rv[x + 2, y + 2] = jnp.where(live, spread_lanes(lambda t: tiles[t], y, lane), 0.0)
        return carry

    walk(0, XC, lay_out, 0, 4)
    take_d.wait()
    pl.semaphore_wait(barrier, len(near))

    heat, dens = [], []
    for k, (dx, dy) in enumerate(SIDES):
        copy = pltpu.make_async_remote_copy(
            src_ref=dd.at[pl.ds(*DENS_FROM[dx]), pl.ds(*DENSY_FROM[dy])],
            dst_ref=dd.at[pl.ds(*DENS_TO[dx]), pl.ds(*DENSY_TO[dy])],
            send_sem=dens_send.at[k],
            recv_sem=dens_recv.at[k],
            device_id=beside[k],
            device_id_type=MESH,
        )
        copy.start()
        dens.append(copy)
    for k, (dx, dy) in enumerate(SIDES):
        copy = pltpu.make_async_remote_copy(
            src_ref=rv.at[pl.ds(*HEAT_FROM[dx]), pl.ds(*HEATY_FROM[dy])],
            dst_ref=rv.at[pl.ds(*HEAT_TO[dx]), pl.ds(*HEATY_TO[dy])],
            send_sem=heat_send.at[k],
            recv_sem=heat_recv.at[k],
            device_id=beside[k],
            device_id_type=MESH,
        )
        copy.start()
        heat.append(copy)

    tell(0)

    hear(0)
    tell(1)
    for copy in dens:
        copy.wait_recv()
    for octet in range(4):
        x = sub + (8 * octet - 8)
        x_in = ((x >= 0) | (ix > 0)) & ((x < XC) | (ix < gxn - 1)) & live
        for ey in range(13):
            flat = spread_lanes(
                lambda t, octet=octet: dd[pl.ds(8 * octet, 8), pl.ds(LANES * t, LANES)], ey + 1, lane
            )
            y = ey - 3
            inside = x_in
            if y < 0:
                inside = inside & (iy > 0)
            if y >= YC:
                inside = inside & (iy < gyn - 1)
            c = KMIN + (1.0 - KMIN) * (flat * flat * flat)
            cu[ey, pl.ds(8 * octet, 8), :] = jnp.where(inside, c * (1.0 / 24.0), 0.0)
    lane32 = lax.broadcasted_iota(jnp.int32, (32, LANES), 1)
    x32 = lax.broadcasted_iota(jnp.int32, (32, LANES), 0) - 8
    x_in32 = ((x32 >= 0) | (ix > 0)) & ((x32 < XC) | (ix < gxn - 1)) & (lane32 < NZ)
    for ny in range(YN):
        both = cu[ny] + cu[ny + 1]
        both = both + pltpu.roll(both, 1, 1)
        both = 8.0 * (both + pltpu.roll(both, 1, 0))
        inside = x_in32
        if ny < 2:
            inside = inside & (iy > 0)
        if ny >= YC + 2:
            inside = inside & (iy < gyn - 1)
        mi[ny] = jnp.where(inside, 1.0 / both, 0.0)

    zero = jnp.zeros((LOADS, LANES), jnp.float32)

    def first_moment(x, s0):
        terms = []
        for y in range(YC):
            r = rv[x + 2, y + 2]
            terms.append(r * (r * row_of(mi, y + 2, x + 8)))
        return s0 + tree(terms)

    s0 = walk(0, XC, first_moment, zero, 2)
    for k in range(1, count - 1):
        hear(k)
        tell(k + 1)
    for copy in heat:
        copy.wait_recv()

    def scaled_row(i):
        out = []
        for y in range(YN):
            z = rv[i, y] * row_of(mi, y, i + 6)
            zv[i, y] = z
            out.append(z)
        return out

    def emit_image(i, sums, extra):
        for y, off in enumerate(sums):
            q = rv[i, y + 1] + off
            qv[i - 1, y] = q
            yv[i - 1, y] = q * row_of(mi, y + 1, i + 6)
        return extra

    apply_rows(scaled_row, lambda i, y: row_of(cu, y + 1, i + 6), XN, emit_image, 0, BY_IMAGE)

    def emit_second(i, sums, extra):
        terms = [[], [], []]
        for y, off in enumerate(sums):
            q = qv[i, y + 1]
            yy = yv[i, y + 1]
            p = q + off
            pv[i - 1, y] = p
            for some, term in zip(terms, (zv[i + 1, y + 2] * q, yy * q, yy * p)):
                some.append(term)
        return tuple(e + tree(t) for e, t in zip(extra, terms))

    moments = apply_rows(
        lambda i: [yv[i, y] for y in range(YC + 2)],
        lambda i, y: row_of(cu, y + 2, i + 7),
        XC + 2,
        emit_second,
        (zero,) * 3,
        BY_SECOND,
    )
    moments = (s0,) + tuple(moments)
    hear(count - 1)

    spot = zero
    for k in range(4):
        total = jnp.sum(moments[k], axis=1, keepdims=True)
        spot = spot + jnp.where(lane == 4 * sub + k, total, 0.0)
    rows[0] = jnp.sum(spot, axis=0, keepdims=True)
    def pack(x, carry):
        for ref, out, dx, dy in ((zv, zp, 2, 2), (yv, yp, 1, 1), (qv, qp, 1, 1), (pv, pp, 0, 0)):
            for part in range(2):
                cols = [ref[x + dx, 4 * part + k + dy] for k in range(4)]
                for t, tile in enumerate(pack_lanes(cols, lane)):
                    out[pl.ds(tile_row(x, 3 * part + t), LOADS, stride=TILE_STEP), :] = tile
        return carry

    sent = []
    done = 0
    for step, group in enumerate(groups):
        copies = []
        for r, one in enumerate(group):
            copies.append(
                pltpu.make_async_remote_copy(
                    src_ref=rows.at[step],
                    dst_ref=got.at[done + r],
                    send_sem=sum_send.at[done + r],
                    recv_sem=sum_recv.at[done + r],
                    device_id=one,
                    device_id_type=MESH,
                )
            )
        for copy in copies:
            copy.start()
        if step == len(groups) - 1:
            walk(0, XC, pack, 0, 2)
        for copy in reversed(copies):
            copy.wait_recv()
        rows[step + 1] = tree([rows[step]] + [got[done + r] for r in reversed(range(len(copies)))])
        done += len(copies)
        sent += copies

    whole = jnp.broadcast_to(rows[len(groups)], (LOADS, LANES))
    s0, s1, s2, s3 = [
        jnp.sum(jnp.where(lane == 4 * sub + k, whole, 0.0), axis=1, keepdims=True) for k in range(4)
    ]
    a0 = s0 / s1
    g = s2 / s1
    mu = (a0 * g - 1.0) / (s3 / s1 - g * g)
    first = a0 + mu * g
    for load in range(LOADS):
        f = jnp.broadcast_to(first[load : load + 1], (LOADS, LANES))
        m = jnp.broadcast_to(mu[load : load + 1], (LOADS, LANES))
        at = [pl.ds(load * TILE_STEP + 8 * t, 8) for t in range(TILE_STEP // 8)]
        xs = [f * zp[a, :] - m * yp[a, :] for a in at]
        rs = [(hv[a, :] - f * qp[a, :]) + m * pp[a, :] for a in at]
        for a, x, r in zip(at, xs, rs):
            x_out[a, :] = x
            r_out[a, :] = r
    for copy in dens + heat + sent:
        copy.wait_send()


def put_out(x, r, x_out, r_out, sem):
    copies = [pltpu.make_async_copy(x, x_out, sem.at[0]), pltpu.make_async_copy(r, r_out, sem.at[1])]
    for copy in copies:
        copy.start()
    for copy in copies:
        copy.wait()


def solution(mesh):
    gxn, gyn = mesh.shape["gx"], mesh.shape["gy"]
    lown = 8 if gyn % 8 == 0 and gyn > 8 else 2
    hin = gyn // lown
    count = sum(math.prod(t) - 1 for t in turns_of(lown // 2, hin, gxn))

    def per_device(heat_source, density):
        loads, xc, flat = heat_source.shape
        out = jax.ShapeDtypeStruct((loads * xc * flat // LANES, LANES), jnp.float32)
        f32 = jnp.float32
        dma = pltpu.SemaphoreType.DMA
        sol, res = pl.pallas_call(
            functools.partial(kernel, gxn, lown, hin),
            out_shape=(out, out),
            in_specs=[pl.BlockSpec(memory_space=pltpu.HBM)] * 2,
            out_specs=[pl.BlockSpec(memory_space=pltpu.VMEM)] * 2,
            scratch_shapes=[
                pltpu.VMEM((LOADS * TILE_STEP, LANES), f32),
                pltpu.VMEM((32, 1408), f32),
                pltpu.VMEM((XN, YN, LOADS, LANES), f32),
                pltpu.VMEM((XN, YN, LOADS, LANES), f32),
                pltpu.VMEM((XC + 2, YC + 2, LOADS, LANES), f32),
                pltpu.VMEM((XC + 2, YC + 2, LOADS, LANES), f32),
                pltpu.VMEM((XC, YC, LOADS, LANES), f32),
                pltpu.VMEM((LOADS * TILE_STEP, LANES), f32),
                pltpu.VMEM((LOADS * TILE_STEP, LANES), f32),
                pltpu.VMEM((LOADS * TILE_STEP, LANES), f32),
                pltpu.VMEM((LOADS * TILE_STEP, LANES), f32),
                pltpu.VMEM((13, 32, LANES), f32),
                pltpu.VMEM((YN, 32, LANES), f32),
                pltpu.VMEM((4, 1, LANES), f32),
                pltpu.VMEM((count, 1, LANES), f32),
                dma((2,)),
                dma((8,)),
                dma((8,)),
                dma((8,)),
                dma((8,)),
                dma((count,)),
                dma((count,)),
                pltpu.SemaphoreType.REGULAR((len(hops(hin, 0)) + len(hops(gxn, 1)),)),
            ],
            compiler_params=pltpu.CompilerParams(
                collective_id=0, has_side_effects=True, vmem_limit_bytes=GRANT
            ),
            name="two_steps",
        )(to_tiles(heat_source), density)
        sol, res = pl.pallas_call(
            put_out,
            out_shape=(out, out),
            in_specs=[pl.BlockSpec(memory_space=pltpu.VMEM)] * 2,
            out_specs=[pl.BlockSpec(memory_space=pltpu.HBM)] * 2,
            scratch_shapes=[dma((2,))],
            compiler_params=pltpu.CompilerParams(vmem_limit_bytes=2 * 1024 * 1024),
            name="put_out",
        )(sol, res)
        return from_tiles(sol), from_tiles(res)

    placed = P(None, "gx", "gy")
    return jax.shard_map(
        per_device,
        mesh=mesh,
        in_specs=(placed, P("gx", "gy")),
        out_specs=(placed, placed),
        check_vma=False,
    )
```

```python
import functools
import math

import jax
import jax.numpy as jnp
from jax import lax
from jax.experimental import pallas as pl
from jax.experimental.pallas import tpu as pltpu
from jax.sharding import PartitionSpec as P

NZ = 96
KMIN = 0.001
MESH = pl.DeviceIdType.MESH
LANES = 128
GRANT = 53 * 1024 * 1024
BY_IMAGE, BY_SECOND = 6, 8
LOADS = 8
XC = 16
YC = 8
XN, YN = XC + 4, YC + 4
SIDES = [(dx, dy) for dx in (-1, 0, 1) for dy in (-1, 0, 1) if (dx, dy) != (0, 0)]

HEAT_FROM = {1: (XC, 2), 0: (2, XC), -1: (2, 2)}
HEAT_TO = {1: (0, 2), 0: (2, XC), -1: (XC + 2, 2)}
HEATY_FROM = {1: (YC, 2), 0: (2, YC), -1: (2, 2)}
HEATY_TO = {1: (0, 2), 0: (2, YC), -1: (YC + 2, 2)}
HALF = XC // 2
HEAT_PARTS = (
    [(0, dy, (2, HALF), (2, HALF)) for dy in (-1, 1)]
    + [(1, dy, HEAT_FROM[1], HEAT_TO[1]) for dy in (0, -1, 1)]
    + [(0, dy, (2 + HALF, HALF), (2 + HALF, HALF)) for dy in (-1, 1)]
    + [(-1, dy, HEAT_FROM[-1], HEAT_TO[-1]) for dy in (0, -1, 1)]
)
EARLY = 5
DENS_FROM = {1: (16, 8), 0: (8, 16), -1: (8, 8)}
DENS_TO = {1: (0, 8), 0: (8, 16), -1: (24, 8)}
DENSY_FROM = {1: (768, 384), 0: (384, 768), -1: (384, 256)}
DENSY_TO = {1: (0, 384), 0: (384, 768), -1: (1152, 256)}


TILES = YC * NZ // LANES
TILE_STEP = XC * TILES

PARTS = [pl.ds(k * LOADS * TILE_STEP // 4, LOADS * TILE_STEP // 4) for k in range(4)]


def to_tiles(field):
    parts = field.reshape(LOADS, XC // 8, 8, TILES, LANES)
    return parts.transpose(0, 1, 3, 2, 4).reshape(LOADS * TILE_STEP, LANES)


def from_tiles(rows):
    parts = rows.reshape(LOADS, XC // 8, TILES, 8, LANES)
    return parts.transpose(0, 1, 3, 2, 4).reshape(LOADS, XC, TILES * LANES)


def tile_row(x, tile):
    return (x // 8) * (8 * TILES) + lax.rem(x, 8) + 8 * tile


def spread_lanes(tile_of, y, lane):
    first = (y * NZ) // LANES
    kind = y % 4
    if kind == 0:
        return tile_of(first)
    if kind == 1:
        return pltpu.roll(jnp.where(lane >= 96, tile_of(first), tile_of(first + 1)), 32, 1)
    if kind == 2:
        return pltpu.roll(jnp.where(lane >= 64, tile_of(first), tile_of(first + 1)), 64, 1)
    return pltpu.roll(tile_of(first), 96, 1)


def pack_lanes(cols, lane):
    one = pltpu.roll(cols[1], 96, 1)
    two = pltpu.roll(cols[2], 64, 1)
    three = pltpu.roll(cols[3], 32, 1)
    return (
        jnp.where(lane < 96, cols[0], one),
        jnp.where(lane < 64, one, two),
        jnp.where(lane < 32, two, three),
    )


def row_of(ref, col, row):
    return jnp.broadcast_to(ref[col, pl.ds(row, 1), :], (LOADS, LANES))


def row_fields(tiles):
    ups = [pltpu.roll(t, LANES - 1, 1) for t in tiles]
    s = [t + u for t, u in zip(tiles, ups)]
    d = [t - u for t, u in zip(tiles, ups)]
    return s, d, [s[y] + s[y + 1] for y in range(len(s) - 1)]


def element_row(low, high, coef):
    s0, d0, p0 = low
    s1, d1, p1 = high
    ct, c1, c2, cq, cp = [[] for _ in range(5)]
    for y in range(len(s0) - 1):
        c = coef(y)
        ct.append(c * (p0[y] + p1[y]))
        c1.append(c * (s0[y] - s1[y + 1]))
        c2.append(c * (s0[y + 1] - s1[y]))
        cq.append(c * (d0[y + 1] + d1[y]))
        cp.append(c * (d0[y] + d1[y + 1]))
    inner = range(1, len(s0) - 1)
    u = [ct[y] + ct[y - 1] for y in inner]
    below = (
        [(c1[y] + c2[y - 1]) - u[y - 1] for y in inner],
        [cq[y] + cp[y - 1] for y in inner],
    )
    above = (
        [(c1[y - 1] + c2[y]) + u[y - 1] for y in inner],
        [cq[y - 1] + cp[y] for y in inner],
    )
    return below, above


def apply_rows(load_row, coef_at, rows, emit, start, by, between=None):
    first_row = row_fields(load_row(0))
    second = row_fields(load_row(1))
    _, above = element_row(first_row, second, lambda y: coef_at(0, y))

    def body(i, carry):
        low, (tops, topd), extra = carry
        high = row_fields(load_row(i + 1))
        (bots, botd), above = element_row(low, high, lambda y: coef_at(i, y))
        sums = []
        for k in range(len(bots)):
            n_s = bots[k] - tops[k]
            n_d = botd[k] + topd[k]
            sums.append((n_s + n_d) + pltpu.roll(n_s - n_d, 1, 1))
        return high, above, emit(i, sums, extra)

    carry, at = (second, above, start), 1
    if between is not None:
        carry, at = walk(1, 1 + by, body, carry, by), 1 + by
        between()
    return walk(at, rows - 1, body, carry, by)[2]


def walk(start, stop, body, carry, by):
    def turn(t, carry):
        for k in range(by):
            carry = body(start + t * by + k, carry)
        return carry

    turns = (stop - start) // by
    if turns == 1:
        for k in range(by):
            carry = body(start + k, carry)
        return carry
    return lax.fori_loop(0, turns, turn, carry)


def tree(terms):
    while len(terms) > 1:
        pairs = [terms[k] + terms[k + 1] for k in range(0, len(terms) - 1, 2)]
        terms = pairs + terms[len(terms) - len(terms) % 2 :]
    return terms[0]


def wrap(i, n):
    return jnp.where(i >= n, i - n, i)


def hops(n, known):
    ahead, out = 1 - known, []
    while known < n // 2:
        step = min(known + ahead, n // 2 - known)
        out.append(step)
        known += step
    return out


def turns_of(xn, yn, zn):
    return [(1, 1, zn, 2), (xn, yn, 1, 1)]


def kernel(
    gxn, lown, hin, h_hbm, d_hbm, x_out, r_out,
    hv, dd, rv, zv, qv, yv, pv, zp, yp, qp, pp, cu, mi, rows, got,
    in_sem, heat_send, heat_recv, dens_send, dens_recv, sum_send, sum_recv, known,
):
    gyn = lown * hin
    ix, iy = lax.axis_index("gx"), lax.axis_index("gy")
    hi = iy // lown
    lo = iy - hi * lown
    xs_at = {d: wrap(ix + (d + gxn if d < 0 else d), gxn) for d in (-1, 0, 1)}
    ys_at = {d: wrap(iy + (d + gyn if d < 0 else d), gyn) for d in (-1, 0, 1)}
    xs_at[0], ys_at[0] = ix, iy
    beside = [(xs_at[dx], ys_at[dy]) for dx, dy in SIDES]
    rings = [
        [(ix, hi * lown + wrap(lo + r, lown)) for r in range(1, lown)],
        [(ix, wrap(hi + r, hin) * lown + lo) for r in range(1, hin)],
        [(wrap(ix + r, gxn), iy) for r in range(1, gxn)],
    ]
    core = lo - 2 * (lo // 2)
    groups = []
    for xs, ys, zs, cores in turns_of(lown // 2, hin, gxn):
        group = []
        for dx in range(xs):
            for dy in range(ys):
                for dz in range(zs):
                    for dc in range(cores):
                        far = sum(min(d, n - d) for d, n in ((dx, xs), (dy, ys), (dz, zs)))
                        if far + dc == 0:
                            continue
                        at = wrap(lo + 2 * dx, lown)
                        if dc:
                            at = at + 1 - 2 * core
                        group.append((-far, (wrap(ix + dz, gxn), wrap(hi + dy, hin) * lown + at)))
        groups.append([one for _, one in sorted(group, key=lambda g: g[0])])
    near = beside + rings[0] + [rings[1][0], rings[1][-1]]

    barrier = pltpu.get_barrier_semaphore()
    for one in near:
        pl.semaphore_signal(barrier, inc=1, device_id=one, device_id_type=MESH)
    turns = []
    for ring, n, known_at in ((rings[1], hin, 0), (rings[2], gxn, 1)):
        turns.append([(ring[d - 1], ring[n - 1 - d]) for d in hops(n, known_at)])
    count = max(len(t) for t in turns)
    turns = [[t[k] for t in turns if k < len(t)] for k in range(count)]
    flat_turns = [(k, pair) for k, pairs in enumerate(turns) for pair in pairs]

    def tell(k):
        for at, (turn, pair) in enumerate(flat_turns):
            if turn == k:
                for one in pair:
                    pl.semaphore_signal(known.at[at], inc=1, device_id=one, device_id_type=MESH)

    def hear(k):
        for at, (turn, _) in enumerate(flat_turns):
            if turn == k:
                pl.semaphore_wait(known.at[at], 2)

    take_d = pltpu.make_async_copy(d_hbm, dd.at[pl.ds(8, 16), pl.ds(384, 768)], in_sem.at[len(PARTS)])
    take_h = [pltpu.make_async_copy(h_hbm.at[part], hv.at[part], in_sem.at[k]) for k, part in enumerate(PARTS)]
    for copy in take_h:
        copy.start()
    take_d.start()
    lane = lax.broadcasted_iota(jnp.int32, (LOADS, LANES), 1)
    sub = lax.broadcasted_iota(jnp.int32, (LOADS, LANES), 0)
    live = lane < NZ
    for copy in take_h:
        copy.wait()

    def lay_out(x, carry):
        tiles = [hv[pl.ds(tile_row(x, t), LOADS, stride=TILE_STEP), :] for t in range(6)]
        for y in range(YC):
            rv[x + 2, y + 2] = jnp.where(live, spread_lanes(lambda t: tiles[t], y, lane), 0.0)
        return carry

    walk(0, XC, lay_out, 0, 4)
    take_d.wait()
    pl.semaphore_wait(barrier, len(near))

    heat, dens = [], []
    for k, (dx, dy) in enumerate(SIDES):
        copy = pltpu.make_async_remote_copy(
            src_ref=dd.at[pl.ds(*DENS_FROM[dx]), pl.ds(*DENSY_FROM[dy])],
            dst_ref=dd.at[pl.ds(*DENS_TO[dx]), pl.ds(*DENSY_TO[dy])],
            send_sem=dens_send.at[k],
            recv_sem=dens_recv.at[k],
            device_id=beside[k],
            device_id_type=MESH,
        )
        copy.start()
        dens.append(copy)
    for k, (dx, dy, from_x, to_x) in enumerate(HEAT_PARTS):
        copy = pltpu.make_async_remote_copy(
            src_ref=rv.at[pl.ds(*from_x), pl.ds(*HEATY_FROM[dy])],
            dst_ref=rv.at[pl.ds(*to_x), pl.ds(*HEATY_TO[dy])],
            send_sem=heat_send.at[k],
            recv_sem=heat_recv.at[k],
            device_id=beside[SIDES.index((dx, dy))],
            device_id_type=MESH,
        )
        copy.start()
        heat.append(copy)

    tell(0)

    hear(0)
    tell(1)
    for copy in dens:
        copy.wait_recv()
    for octet in range(4):
        x = sub + (8 * octet - 8)
        x_in = ((x >= 0) | (ix > 0)) & ((x < XC) | (ix < gxn - 1)) & live
        for ey in range(13):
            flat = spread_lanes(
                lambda t, octet=octet: dd[pl.ds(8 * octet, 8), pl.ds(LANES * t, LANES)], ey + 1, lane
            )
            y = ey - 3
            inside = x_in
            if y < 0:
                inside = inside & (iy > 0)
            if y >= YC:
                inside = inside & (iy < gyn - 1)
            c = KMIN + (1.0 - KMIN) * (flat * flat * flat)
            cu[ey, pl.ds(8 * octet, 8), :] = jnp.where(inside, c * (1.0 / 24.0), 0.0)
    lane32 = lax.broadcasted_iota(jnp.int32, (32, LANES), 1)
    x32 = lax.broadcasted_iota(jnp.int32, (32, LANES), 0) - 8
    x_in32 = ((x32 >= 0) | (ix > 0)) & ((x32 < XC) | (ix < gxn - 1)) & (lane32 < NZ)
    for ny in range(YN):
        both = cu[ny] + cu[ny + 1]
        both = both + pltpu.roll(both, 1, 1)
        both = 8.0 * (both + pltpu.roll(both, 1, 0))
        inside = x_in32
        if ny < 2:
            inside = inside & (iy > 0)
        if ny >= YC + 2:
            inside = inside & (iy < gyn - 1)
        mi[ny] = jnp.where(inside, 1.0 / both, 0.0)

    zero = jnp.zeros((LOADS, LANES), jnp.float32)

    def first_moment(x, s0):
        terms = []
        for y in range(YC):
            r = rv[x + 2, y + 2]
            terms.append(r * (r * row_of(mi, y + 2, x + 8)))
        return s0 + tree(terms)

    s0 = walk(0, XC, first_moment, zero, 2)
    for k in range(1, count - 1):
        hear(k)
        tell(k + 1)
    for copy in heat[:EARLY]:
        copy.wait_recv()

    def wait_rest():
        for copy in heat[EARLY:]:
            copy.wait_recv()


    def scaled_row(i):
        out = []
        for y in range(YN):
            z = rv[i, y] * row_of(mi, y, i + 6)
            zv[i, y] = z
            out.append(z)
        return out

    def emit_image(i, sums, extra):
        for y, off in enumerate(sums):
            q = rv[i, y + 1] + off
            qv[i - 1, y] = q
            yv[i - 1, y] = q * row_of(mi, y + 1, i + 6)
        return extra

    apply_rows(scaled_row, lambda i, y: row_of(cu, y + 1, i + 6), XN, emit_image, 0, BY_IMAGE, wait_rest)

    def emit_second(i, sums, extra):
        terms = [[], [], []]
        for y, off in enumerate(sums):
            q = qv[i, y + 1]
            yy = yv[i, y + 1]
            p = q + off
            pv[i - 1, y] = p
            for some, term in zip(terms, (zv[i + 1, y + 2] * q, yy * q, yy * p)):
                some.append(term)
        return tuple(e + tree(t) for e, t in zip(extra, terms))

    moments = apply_rows(
        lambda i: [yv[i, y] for y in range(YC + 2)],
        lambda i, y: row_of(cu, y + 2, i + 7),
        XC + 2,
        emit_second,
        (zero,) * 3,
        BY_SECOND,
    )
    moments = (s0,) + tuple(moments)
    hear(count - 1)

    spot = zero
    for k in range(4):
        total = jnp.sum(moments[k], axis=1, keepdims=True)
        spot = spot + jnp.where(lane == 4 * sub + k, total, 0.0)
    rows[0] = jnp.sum(spot, axis=0, keepdims=True)
    def pack(x, carry):
        for ref, out, dx, dy in ((zv, zp, 2, 2), (yv, yp, 1, 1), (qv, qp, 1, 1), (pv, pp, 0, 0)):
            for part in range(2):
                cols = [ref[x + dx, 4 * part + k + dy] for k in range(4)]
                for t, tile in enumerate(pack_lanes(cols, lane)):
                    out[pl.ds(tile_row(x, 3 * part + t), LOADS, stride=TILE_STEP), :] = tile
        return carry

    sent = []
    done = 0
    for step, group in enumerate(groups):
        copies = []
        for r, one in enumerate(group):
            copies.append(
                pltpu.make_async_remote_copy(
                    src_ref=rows.at[step],
                    dst_ref=got.at[done + r],
                    send_sem=sum_send.at[done + r],
                    recv_sem=sum_recv.at[done + r],
                    device_id=one,
                    device_id_type=MESH,
                )
            )
        for copy in copies:
            copy.start()
        if step == len(groups) - 1:
            walk(0, XC, pack, 0, 2)
        for copy in reversed(copies):
            copy.wait_recv()
        rows[step + 1] = tree([rows[step]] + [got[done + r] for r in reversed(range(len(copies)))])
        done += len(copies)
        sent += copies

    whole = jnp.broadcast_to(rows[len(groups)], (LOADS, LANES))
    s0, s1, s2, s3 = [
        jnp.sum(jnp.where(lane == 4 * sub + k, whole, 0.0), axis=1, keepdims=True) for k in range(4)
    ]
    a0 = s0 / s1
    g = s2 / s1
    mu = (a0 * g - 1.0) / (s3 / s1 - g * g)
    first = a0 + mu * g
    for load in range(LOADS):
        f = jnp.broadcast_to(first[load : load + 1], (LOADS, LANES))
        m = jnp.broadcast_to(mu[load : load + 1], (LOADS, LANES))
        at = [pl.ds(load * TILE_STEP + 8 * t, 8) for t in range(TILE_STEP // 8)]
        xs = [f * zp[a, :] - m * yp[a, :] for a in at]
        rs = [(hv[a, :] - f * qp[a, :]) + m * pp[a, :] for a in at]
        for a, x, r in zip(at, xs, rs):
            x_out[a, :] = x
            r_out[a, :] = r
    for copy in dens + heat + sent:
        copy.wait_send()


def put_out(x, r, x_out, r_out, sem):
    copies = [
        pltpu.make_async_copy(a.at[part], b.at[part], sem.at[i, k])
        for k, part in enumerate(PARTS)
        for i, (a, b) in enumerate(((x, x_out), (r, r_out)))
    ]
    for copy in copies:
        copy.start()
    for copy in copies:
        copy.wait()


def solution(mesh):
    gxn, gyn = mesh.shape["gx"], mesh.shape["gy"]
    lown = 8 if gyn % 8 == 0 and gyn > 8 else 2
    hin = gyn // lown
    count = sum(math.prod(t) - 1 for t in turns_of(lown // 2, hin, gxn))

    def per_device(heat_source, density):
        loads, xc, flat = heat_source.shape
        out = jax.ShapeDtypeStruct((loads * xc * flat // LANES, LANES), jnp.float32)
        f32 = jnp.float32
        dma = pltpu.SemaphoreType.DMA
        sol, res = pl.pallas_call(
            functools.partial(kernel, gxn, lown, hin),
            out_shape=(out, out),
            in_specs=[pl.BlockSpec(memory_space=pltpu.HBM)] * 2,
            out_specs=[pl.BlockSpec(memory_space=pltpu.VMEM)] * 2,
            scratch_shapes=[
                pltpu.VMEM((LOADS * TILE_STEP, LANES), f32),
                pltpu.VMEM((32, 1408), f32),
                pltpu.VMEM((XN, YN, LOADS, LANES), f32),
                pltpu.VMEM((XN, YN, LOADS, LANES), f32),
                pltpu.VMEM((XC + 2, YC + 2, LOADS, LANES), f32),
                pltpu.VMEM((XC + 2, YC + 2, LOADS, LANES), f32),
                pltpu.VMEM((XC, YC, LOADS, LANES), f32),
                pltpu.VMEM((LOADS * TILE_STEP, LANES), f32),
                pltpu.VMEM((LOADS * TILE_STEP, LANES), f32),
                pltpu.VMEM((LOADS * TILE_STEP, LANES), f32),
                pltpu.VMEM((LOADS * TILE_STEP, LANES), f32),
                pltpu.VMEM((13, 32, LANES), f32),
                pltpu.VMEM((YN, 32, LANES), f32),
                pltpu.VMEM((4, 1, LANES), f32),
                pltpu.VMEM((count, 1, LANES), f32),
                dma((len(PARTS) + 1,)),
                dma((len(HEAT_PARTS),)),
                dma((len(HEAT_PARTS),)),
                dma((8,)),
                dma((8,)),
                dma((count,)),
                dma((count,)),
                pltpu.SemaphoreType.REGULAR((len(hops(hin, 0)) + len(hops(gxn, 1)),)),
            ],
            compiler_params=pltpu.CompilerParams(
                collective_id=0, has_side_effects=True, vmem_limit_bytes=GRANT
            ),
            name="two_steps",
        )(to_tiles(heat_source), density)
        sol, res = pl.pallas_call(
            put_out,
            out_shape=(out, out),
            in_specs=[pl.BlockSpec(memory_space=pltpu.VMEM)] * 2,
            out_specs=[pl.BlockSpec(memory_space=pltpu.HBM)] * 2,
            scratch_shapes=[dma((2, len(PARTS)))],
            compiler_params=pltpu.CompilerParams(vmem_limit_bytes=2 * 1024 * 1024),
            name="put_out",
        )(sol, res)
        return from_tiles(sol), from_tiles(res)

    placed = P(None, "gx", "gy")
    return jax.shard_map(
        per_device,
        mesh=mesh,
        in_specs=(placed, P("gx", "gy")),
        out_specs=(placed, placed),
        check_vma=False,
    )
```

```python
import functools
import math

import jax
import jax.numpy as jnp
from jax import lax
from jax.experimental import pallas as pl
from jax.experimental.pallas import tpu as pltpu
from jax.sharding import PartitionSpec as P

NZ = 96
KMIN = 0.001
MESH = pl.DeviceIdType.MESH
LANES = 128
GRANT = 53 * 1024 * 1024
BY_IMAGE, BY_SECOND = 6, 8
LOADS = 8
XC = 16
YC = 8
XN, YN = XC + 4, YC + 4
SIDES = [(dx, dy) for dx in (-1, 0, 1) for dy in (-1, 0, 1) if (dx, dy) != (0, 0)]

HEAT_FROM = {1: (XC, 2), 0: (2, XC), -1: (2, 2)}
HEAT_TO = {1: (0, 2), 0: (2, XC), -1: (XC + 2, 2)}
HEATY_FROM = {1: (YC, 2), 0: (2, YC), -1: (2, 2)}
HEATY_TO = {1: (0, 2), 0: (2, YC), -1: (YC + 2, 2)}
HALF = XC // 2
HEAT_PARTS = (
    [(0, dy, (2, HALF), (2, HALF)) for dy in (-1, 1)]
    + [(1, dy, HEAT_FROM[1], HEAT_TO[1]) for dy in (0, -1, 1)]
    + [(0, dy, (2 + HALF, HALF), (2 + HALF, HALF)) for dy in (-1, 1)]
    + [(-1, dy, HEAT_FROM[-1], HEAT_TO[-1]) for dy in (0, -1, 1)]
)
EARLY = 5
DENS_FROM = {1: (16, 8), 0: (8, 16), -1: (8, 8)}
DENS_TO = {1: (0, 8), 0: (8, 16), -1: (24, 8)}
DENSY_FROM = {1: (768, 384), 0: (384, 768), -1: (384, 256)}
DENSY_TO = {1: (0, 384), 0: (384, 768), -1: (1152, 256)}


TILES = YC * NZ // LANES
TILE_STEP = XC * TILES

PARTS = [pl.ds(k * LOADS * TILE_STEP // 4, LOADS * TILE_STEP // 4) for k in range(4)]


def to_tiles(field):
    parts = field.reshape(LOADS, XC // 8, 8, TILES, LANES)
    return parts.transpose(0, 1, 3, 2, 4).reshape(LOADS * TILE_STEP, LANES)


def from_tiles(rows):
    parts = rows.reshape(LOADS, XC // 8, TILES, 8, LANES)
    return parts.transpose(0, 1, 3, 2, 4).reshape(LOADS, XC, TILES * LANES)


def tile_row(x, tile):
    return (x // 8) * (8 * TILES) + lax.rem(x, 8) + 8 * tile


def spread_lanes(tile_of, y, lane):
    first = (y * NZ) // LANES
    kind = y % 4
    if kind == 0:
        return tile_of(first)
    if kind == 1:
        return pltpu.roll(jnp.where(lane >= 96, tile_of(first), tile_of(first + 1)), 32, 1)
    if kind == 2:
        return pltpu.roll(jnp.where(lane >= 64, tile_of(first), tile_of(first + 1)), 64, 1)
    return pltpu.roll(tile_of(first), 96, 1)


def pack_lanes(cols, lane):
    one = pltpu.roll(cols[1], 96, 1)
    two = pltpu.roll(cols[2], 64, 1)
    three = pltpu.roll(cols[3], 32, 1)
    return (
        jnp.where(lane < 96, cols[0], one),
        jnp.where(lane < 64, one, two),
        jnp.where(lane < 32, two, three),
    )


def row_of(ref, col, row):
    return jnp.broadcast_to(ref[col, pl.ds(row, 1), :], (LOADS, LANES))


def row_fields(tiles):
    ups = [pltpu.roll(t, LANES - 1, 1) for t in tiles]
    s = [t + u for t, u in zip(tiles, ups)]
    d = [t - u for t, u in zip(tiles, ups)]
    return s, d, [s[y] + s[y + 1] for y in range(len(s) - 1)]


def element_row(low, high, coef):
    s0, d0, p0 = low
    s1, d1, p1 = high
    ct, c1, c2, cq, cp = [[] for _ in range(5)]
    for y in range(len(s0) - 1):
        c = coef(y)
        ct.append(c * (p0[y] + p1[y]))
        c1.append(c * (s0[y] - s1[y + 1]))
        c2.append(c * (s0[y + 1] - s1[y]))
        cq.append(c * (d0[y + 1] + d1[y]))
        cp.append(c * (d0[y] + d1[y + 1]))
    inner = range(1, len(s0) - 1)
    u = [ct[y] + ct[y - 1] for y in inner]
    below = (
        [(c1[y] + c2[y - 1]) - u[y - 1] for y in inner],
        [cq[y] + cp[y - 1] for y in inner],
    )
    above = (
        [(c1[y - 1] + c2[y]) + u[y - 1] for y in inner],
        [cq[y - 1] + cp[y] for y in inner],
    )
    return below, above


def apply_rows(load_row, coef_at, rows, emit, start, by, between=None):
    first_row = row_fields(load_row(0))
    second = row_fields(load_row(1))
    _, above = element_row(first_row, second, lambda y: coef_at(0, y))

    def body(i, carry):
        low, (tops, topd), extra = carry
        high = row_fields(load_row(i + 1))
        (bots, botd), above = element_row(low, high, lambda y: coef_at(i, y))
        sums = []
        for k in range(len(bots)):
            n_s = bots[k] - tops[k]
            n_d = botd[k] + topd[k]
            sums.append((n_s + n_d) + pltpu.roll(n_s - n_d, 1, 1))
        return high, above, emit(i, sums, extra)

    carry, at = (second, above, start), 1
    if between is not None:
        carry, at = walk(1, 1 + by, body, carry, by), 1 + by
        between()
    return walk(at, rows - 1, body, carry, by)[2]


def walk(start, stop, body, carry, by):
    def turn(t, carry):
        for k in range(by):
            carry = body(start + t * by + k, carry)
        return carry

    turns = (stop - start) // by
    if turns == 1:
        for k in range(by):
            carry = body(start + k, carry)
        return carry
    return lax.fori_loop(0, turns, turn, carry)


def tree(terms):
    while len(terms) > 1:
        pairs = [terms[k] + terms[k + 1] for k in range(0, len(terms) - 1, 2)]
        terms = pairs + terms[len(terms) - len(terms) % 2 :]
    return terms[0]


def wrap(i, n):
    return jnp.where(i >= n, i - n, i)


def hops(n, known):
    ahead, out = 1 - known, []
    while known < n // 2:
        step = min(known + ahead, n // 2 - known)
        out.append(step)
        known += step
    return out


def turns_of(xn, yn, zn):
    return [(1, 1, zn, 2), (xn, yn, 1, 1)]


def kernel(
    gxn, lown, hin, h_hbm, d_hbm, x_out, r_out,
    hv, dd, rv, zv, qv, yv, pv, zp, yp, qp, pp, cu, mi, rows, got,
    in_sem, heat_send, heat_recv, dens_send, dens_recv, sum_send, sum_recv, known,
):
    gyn = lown * hin
    ix, iy = lax.axis_index("gx"), lax.axis_index("gy")
    hi = iy // lown
    lo = iy - hi * lown
    xs_at = {d: wrap(ix + (d + gxn if d < 0 else d), gxn) for d in (-1, 0, 1)}
    ys_at = {d: wrap(iy + (d + gyn if d < 0 else d), gyn) for d in (-1, 0, 1)}
    xs_at[0], ys_at[0] = ix, iy
    beside = [(xs_at[dx], ys_at[dy]) for dx, dy in SIDES]
    rings = [
        [(ix, hi * lown + wrap(lo + r, lown)) for r in range(1, lown)],
        [(ix, wrap(hi + r, hin) * lown + lo) for r in range(1, hin)],
        [(wrap(ix + r, gxn), iy) for r in range(1, gxn)],
    ]
    core = lo - 2 * (lo // 2)
    groups = []
    for xs, ys, zs, cores in turns_of(lown // 2, hin, gxn):
        group = []
        for dx in range(xs):
            for dy in range(ys):
                for dz in range(zs):
                    for dc in range(cores):
                        far = sum(min(d, n - d) for d, n in ((dx, xs), (dy, ys), (dz, zs)))
                        if far + dc == 0:
                            continue
                        at = wrap(lo + 2 * dx, lown)
                        if dc:
                            at = at + 1 - 2 * core
                        group.append((-far, (wrap(ix + dz, gxn), wrap(hi + dy, hin) * lown + at)))
        groups.append([one for _, one in sorted(group, key=lambda g: g[0])])
    near = beside + rings[0] + [rings[1][0], rings[1][-1]]

    barrier = pltpu.get_barrier_semaphore()
    for one in near:
        pl.semaphore_signal(barrier, inc=1, device_id=one, device_id_type=MESH)
    turns = []
    for ring, n, known_at in ((rings[1], hin, 0), (rings[2], gxn, 1)):
        turns.append([(ring[d - 1], ring[n - 1 - d]) for d in hops(n, known_at)])
    count = max(len(t) for t in turns)
    turns = [[t[k] for t in turns if k < len(t)] for k in range(count)]
    flat_turns = [(k, pair) for k, pairs in enumerate(turns) for pair in pairs]

    def tell(k):
        for at, (turn, pair) in enumerate(flat_turns):
            if turn == k:
                for one in pair:
                    pl.semaphore_signal(known.at[at], inc=1, device_id=one, device_id_type=MESH)

    def hear(k):
        for at, (turn, _) in enumerate(flat_turns):
            if turn == k:
                pl.semaphore_wait(known.at[at], 2)

    take_d = pltpu.make_async_copy(d_hbm, dd.at[pl.ds(8, 16), pl.ds(384, 768)], in_sem.at[len(PARTS)])
    take_h = [pltpu.make_async_copy(h_hbm.at[part], hv.at[part], in_sem.at[k]) for k, part in enumerate(PARTS)]
    for copy in take_h:
        copy.start()
    take_d.start()
    lane = lax.broadcasted_iota(jnp.int32, (LOADS, LANES), 1)
    sub = lax.broadcasted_iota(jnp.int32, (LOADS, LANES), 0)
    live = lane < NZ
    for copy in take_h:
        copy.wait()

    def lay_out(x, carry):
        tiles = [hv[pl.ds(tile_row(x, t), LOADS, stride=TILE_STEP), :] for t in range(6)]
        for y in range(YC):
            rv[x + 2, y + 2] = jnp.where(live, spread_lanes(lambda t: tiles[t], y, lane), 0.0)
        return carry

    walk(0, XC, lay_out, 0, 4)
    take_d.wait()
    pl.semaphore_wait(barrier, len(near))

    heat, dens = [], []
    for k, (dx, dy) in enumerate(SIDES):
        copy = pltpu.make_async_remote_copy(
            src_ref=dd.at[pl.ds(*DENS_FROM[dx]), pl.ds(*DENSY_FROM[dy])],
            dst_ref=dd.at[pl.ds(*DENS_TO[dx]), pl.ds(*DENSY_TO[dy])],
            send_sem=dens_send.at[k],
            recv_sem=dens_recv.at[k],
            device_id=beside[k],
            device_id_type=MESH,
        )
        copy.start()
        dens.append(copy)
    for k, (dx, dy, from_x, to_x) in enumerate(HEAT_PARTS):
        copy = pltpu.make_async_remote_copy(
            src_ref=rv.at[pl.ds(*from_x), pl.ds(*HEATY_FROM[dy])],
            dst_ref=rv.at[pl.ds(*to_x), pl.ds(*HEATY_TO[dy])],
            send_sem=heat_send.at[k],
            recv_sem=heat_recv.at[k],
            device_id=beside[SIDES.index((dx, dy))],
            device_id_type=MESH,
        )
        copy.start()
        heat.append(copy)

    tell(0)

    hear(0)
    tell(1)
    for copy in dens:
        copy.wait_recv()
    for octet in range(4):
        x = sub + (8 * octet - 8)
        x_in = ((x >= 0) | (ix > 0)) & ((x < XC) | (ix < gxn - 1)) & live
        for ey in range(13):
            flat = spread_lanes(
                lambda t, octet=octet: dd[pl.ds(8 * octet, 8), pl.ds(LANES * t, LANES)], ey + 1, lane
            )
            y = ey - 3
            inside = x_in
            if y < 0:
                inside = inside & (iy > 0)
            if y >= YC:
                inside = inside & (iy < gyn - 1)
            c = KMIN + (1.0 - KMIN) * (flat * flat * flat)
            cu[ey, pl.ds(8 * octet, 8), :] = jnp.where(inside, c * (1.0 / 24.0), 0.0)
    lane32 = lax.broadcasted_iota(jnp.int32, (32, LANES), 1)
    x32 = lax.broadcasted_iota(jnp.int32, (32, LANES), 0) - 8
    x_in32 = ((x32 >= 0) | (ix > 0)) & ((x32 < XC) | (ix < gxn - 1)) & (lane32 < NZ)
    for ny in range(YN):
        both = cu[ny] + cu[ny + 1]
        both = both + pltpu.roll(both, 1, 1)
        both = 8.0 * (both + pltpu.roll(both, 1, 0))
        inside = x_in32
        if ny < 2:
            inside = inside & (iy > 0)
        if ny >= YC + 2:
            inside = inside & (iy < gyn - 1)
        mi[ny] = jnp.where(inside, 1.0 / both, 0.0)

    zero = jnp.zeros((LOADS, LANES), jnp.float32)

    def first_moment(x, s0):
        terms = []
        for y in range(YC):
            r = rv[x + 2, y + 2]
            terms.append(r * (r * row_of(mi, y + 2, x + 8)))
        return s0 + tree(terms)

    s0 = walk(0, XC, first_moment, zero, 2)
    for k in range(1, count - 1):
        hear(k)
        tell(k + 1)
    for copy in heat[:EARLY]:
        copy.wait_recv()

    def wait_rest():
        for copy in heat[EARLY:]:
            copy.wait_recv()


    def scaled_row(i):
        out = []
        for y in range(YN):
            z = rv[i, y] * row_of(mi, y, i + 6)
            zv[i, y] = z
            out.append(z)
        return out

    def emit_image(i, sums, extra):
        for y, off in enumerate(sums):
            q = rv[i, y + 1] + off
            qv[i - 1, y] = q
            yv[i - 1, y] = q * row_of(mi, y + 1, i + 6)
        return extra

    apply_rows(scaled_row, lambda i, y: row_of(cu, y + 1, i + 6), XN, emit_image, 0, BY_IMAGE, wait_rest)

    def emit_second(i, sums, extra):
        terms = [[], [], []]
        for y, off in enumerate(sums):
            q = qv[i, y + 1]
            yy = yv[i, y + 1]
            p = q + off
            pv[i - 1, y] = p
            for some, term in zip(terms, (zv[i + 1, y + 2] * q, yy * q, yy * p)):
                some.append(term)
        return tuple(e + tree(t) for e, t in zip(extra, terms))

    moments = apply_rows(
        lambda i: [yv[i, y] for y in range(YC + 2)],
        lambda i, y: row_of(cu, y + 2, i + 7),
        XC + 2,
        emit_second,
        (zero,) * 3,
        BY_SECOND,
    )
    moments = (s0,) + tuple(moments)
    hear(count - 1)

    spot = zero
    for k in range(4):
        total = jnp.sum(moments[k], axis=1, keepdims=True)
        spot = spot + jnp.where(lane == 4 * sub + k, total, 0.0)
    rows[0] = jnp.sum(spot, axis=0, keepdims=True)
    def pack(x, carry):
        for ref, out, dx, dy in ((zv, zp, 2, 2), (yv, yp, 1, 1), (qv, qp, 1, 1), (pv, pp, 0, 0)):
            for part in range(2):
                cols = [ref[x + dx, 4 * part + k + dy] for k in range(4)]
                for t, tile in enumerate(pack_lanes(cols, lane)):
                    out[pl.ds(tile_row(x, 3 * part + t), LOADS, stride=TILE_STEP), :] = tile
        return carry

    sent = []
    done = 0
    for step, group in enumerate(groups):
        copies = []
        for r, one in enumerate(group):
            copies.append(
                pltpu.make_async_remote_copy(
                    src_ref=rows.at[step],
                    dst_ref=got.at[done + r],
                    send_sem=sum_send.at[done + r],
                    recv_sem=sum_recv.at[done + r],
                    device_id=one,
                    device_id_type=MESH,
                )
            )
        for copy in copies:
            copy.start()
        if step == len(groups) - 1:
            walk(0, XC, pack, 0, 2)
        for copy in reversed(copies):
            copy.wait_recv()
        rows[step + 1] = tree([rows[step]] + [got[done + r] for r in reversed(range(len(copies)))])
        done += len(copies)
        sent += copies

    whole = jnp.broadcast_to(rows[len(groups)], (LOADS, LANES))
    s0, s1, s2, s3 = [
        jnp.sum(jnp.where(lane == 4 * sub + k, whole, 0.0), axis=1, keepdims=True) for k in range(4)
    ]
    a0 = s0 / s1
    g = s2 / s1
    mu = (a0 * g - 1.0) / (s3 / s1 - g * g)
    first = a0 + mu * g
    for load in range(LOADS):
        f = jnp.broadcast_to(first[load : load + 1], (LOADS, LANES))
        m = jnp.broadcast_to(mu[load : load + 1], (LOADS, LANES))
        at = [pl.ds(load * TILE_STEP + 8 * t, 8) for t in range(TILE_STEP // 8)]
        xs = [f * zp[a, :] - m * yp[a, :] for a in at]
        rs = [(hv[a, :] - f * qp[a, :]) + m * pp[a, :] for a in at]
        for a, x, r in zip(at, xs, rs):
            x_out[a, :] = x
            r_out[a, :] = r
    for copy in dens + heat + sent:
        copy.wait_send()


def put_out(x, r, x_out, r_out, sem):
    copies = [
        pltpu.make_async_copy(a.at[part], b.at[part], sem.at[i, k])
        for k, part in enumerate(PARTS)
        for i, (a, b) in enumerate(((x, x_out), (r, r_out)))
    ]
    for copy in copies:
        copy.start()
    for copy in copies:
        copy.wait()


def solution(mesh):
    gxn, gyn = mesh.shape["gx"], mesh.shape["gy"]
    lown = 8 if gyn % 8 == 0 and gyn > 8 else 2
    hin = gyn // lown
    count = sum(math.prod(t) - 1 for t in turns_of(lown // 2, hin, gxn))

    def per_device(heat_source, density):
        loads, xc, flat = heat_source.shape
        out = jax.ShapeDtypeStruct((loads * xc * flat // LANES, LANES), jnp.float32)
        f32 = jnp.float32
        dma = pltpu.SemaphoreType.DMA
        sol, res = pl.pallas_call(
            functools.partial(kernel, gxn, lown, hin),
            out_shape=(out, out),
            in_specs=[pl.BlockSpec(memory_space=pltpu.HBM)] * 2,
            out_specs=[pl.BlockSpec(memory_space=pltpu.VMEM)] * 2,
            scratch_shapes=[
                pltpu.VMEM((LOADS * TILE_STEP, LANES), f32),
                pltpu.VMEM((32, 1408), f32),
                pltpu.VMEM((XN, YN, LOADS, LANES), f32),
                pltpu.VMEM((XN, YN, LOADS, LANES), f32),
                pltpu.VMEM((XC + 2, YC + 2, LOADS, LANES), f32),
                pltpu.VMEM((XC + 2, YC + 2, LOADS, LANES), f32),
                pltpu.VMEM((XC, YC, LOADS, LANES), f32),
                pltpu.VMEM((LOADS * TILE_STEP, LANES), f32),
                pltpu.VMEM((LOADS * TILE_STEP, LANES), f32),
                pltpu.VMEM((LOADS * TILE_STEP, LANES), f32),
                pltpu.VMEM((LOADS * TILE_STEP, LANES), f32),
                pltpu.VMEM((13, 32, LANES), f32),
                pltpu.VMEM((YN, 32, LANES), f32),
                pltpu.VMEM((4, 1, LANES), f32),
                pltpu.VMEM((count, 1, LANES), f32),
                dma((len(PARTS) + 1,)),
                dma((len(HEAT_PARTS),)),
                dma((len(HEAT_PARTS),)),
                dma((8,)),
                dma((8,)),
                dma((count,)),
                dma((count,)),
                pltpu.SemaphoreType.REGULAR((len(hops(hin, 0)) + len(hops(gxn, 1)),)),
            ],
            compiler_params=pltpu.CompilerParams(
                collective_id=0, has_side_effects=True, vmem_limit_bytes=GRANT
            ),
            name="two_steps",
        )(to_tiles(heat_source), pltpu.with_memory_space_constraint(density, pltpu.HBM))
        sol, res = pl.pallas_call(
            put_out,
            out_shape=(out, out),
            in_specs=[pl.BlockSpec(memory_space=pltpu.VMEM)] * 2,
            out_specs=[pl.BlockSpec(memory_space=pltpu.HBM)] * 2,
            scratch_shapes=[dma((2, len(PARTS)))],
            compiler_params=pltpu.CompilerParams(vmem_limit_bytes=2 * 1024 * 1024),
            name="put_out",
        )(sol, res)
        return from_tiles(sol), from_tiles(res)

    placed = P(None, "gx", "gy")
    return jax.shard_map(
        per_device,
        mesh=mesh,
        in_specs=(placed, P("gx", "gy")),
        out_specs=(placed, placed),
        check_vma=False,
    )
```
